32 devices in a mesh: fields: 2 (over x), vel: 8 (over z, y), rows: 2 (over core).
Axes of the slice: x: 2, y: 2, z: 4, core: 2. Of those that a mesh axis runs over, the one named last changes fastest.
Arguments:
- images: float32 [16, 64, 4096], P(('fields', 'vel'), 'rows'), parts along dimension 0, may hold values from -6 to 6
- variance: float32 [16, 64, 4096], P(('fields', 'vel'), 'rows'), parts along dimension 0, may hold values from 0.5 to 2
- spread_kernel: float32 [21, 21], replicated, may hold values from 0.05 to 1
- shifts: int32 [576, 3, 2], P(('fields', 'vel')), parts along dimension 0, may hold values from -16 to 16, as said below
- epoch_owner: int32 [6], P('fields'), parts along dimension 0, may hold values from 0 to 7, as said below
- valid_rows: int32 [6, 2], P('fields'), parts along dimension 0, may hold values from 0 to 64, as said below
Outputs:
- likelihood: float32 [576, 64, 4096], P(('fields', 'vel'), 'rows'), parts along dimension 0
The draws below stay inside these ranges and needn't reach their ends.
There are 2 independent parts, one for each index of `fields`. The reference program is written for one: setup_inputs(seed, part) draws one part's arguments, and reference() takes and returns one part's arrays. A program takes and returns all parts, laid end to end along the dimension named above; an argument that names none is the same for every part. Nothing has to cross between parts.
Inputs may be any that keep to these rules, and one draw needn't show every extreme that they name: `shifts`: each entry lies in -16 to 16; both ends are taken in every draw. `epoch_owner`: the epochs are held by distinct slots. `valid_rows`: in each row the first entry is below the second; the first epoch starts at row 0 and the last ends at row 64.
All inputs are finite; a program needn't handle non-finite values.
Results may differ from the reference program's by a relative error of at most 0.0003.
Values sent between devices are 32-bit elements; how exact they have to be, the bound alone decides.
A program may use at most 128 MiB of HBM per device.

```python
import math
import jax
import jax.numpy as jnp
from jax import lax

COLS = 4096
KSIZE = 21
MAXS = 16
EPOCHS = 3
ROWS = 64
VELOCITIES = 288
SLOTS = 8


def draw_shifts(key, part):
    values = jax.random.randint(key, (VELOCITIES, EPOCHS, 2), -MAXS, MAXS + 1)
    values = values.at[0, EPOCHS - 1].set(MAXS)
    values = values.at[VELOCITIES - 1, 0].set(-MAXS)
    return values.astype(jnp.int32)


def draw_epoch_owner(key, part):
    return jax.random.permutation(key, SLOTS)[:EPOCHS].astype(jnp.int32)


def draw_valid_rows(key, part):
    lower_rows = jax.random.randint(jax.random.fold_in(key, 11), (EPOCHS,), 0, ROWS // 4)
    upper_rows = ROWS - jax.random.randint(jax.random.fold_in(key, 12), (EPOCHS,), 0, ROWS // 4)
    lower_rows = lower_rows.at[0].set(0)
    upper_rows = upper_rows.at[EPOCHS - 1].set(ROWS)
    return jnp.stack([lower_rows, upper_rows], axis=1).astype(jnp.int32)


def block_scale(key, extent, shards, low, high):
    def one(axis_at, blocks):
        heights = jax.random.uniform(jax.random.fold_in(jax.random.fold_in(key, 6), axis_at), (blocks,), jnp.float32, low / len(shards), high / len(shards))
        return jnp.repeat(jnp.exp(heights), extent[axis_at] // blocks).reshape((-1,) + (1,) * (len(extent) - axis_at - 1))

    loudness = one(*shards[0])
    for cut in shards[1:]:
        loudness = loudness * one(*cut)
    return loudness


def normal_values(rng, shape, deviation, most, pieces=(), kind=jnp.bfloat16):
    array = deviation * jax.random.normal(rng, shape, jnp.float32)
    if pieces:
        array = array * block_scale(rng, shape, pieces, -0.22, 0.18)
    return jnp.clip(array, -most, most).astype(kind)


def setup_inputs(seed: int = 0, part: int = 0) -> dict:
    arg_keys = jax.random.split(jax.random.key(seed), 7)
    part_keys = jax.random.split(jax.random.fold_in(arg_keys[6], part), 7)
    images = normal_values(part_keys[0], (SLOTS, ROWS, COLS), 1.0, 6.0, ((0, 8), (1, 2)), jnp.float32)
    variance = jnp.clip(0.5 + 1.5 * jax.random.uniform(part_keys[1], (SLOTS, ROWS, COLS), jnp.float32) ** block_scale(part_keys[1], (SLOTS, ROWS, COLS), ((0, 8), (1, 2)), -0.2, 0.2), 0.5, 2.0)
    spread_kernel = jnp.clip(jnp.exp(jax.random.uniform(arg_keys[2], (KSIZE, KSIZE), jnp.float32, math.log(0.05), math.log(1.0))), 0.05, 1.0)
    shifts = draw_shifts(jax.random.fold_in(jax.random.fold_in(arg_keys[6], part), 71), part)
    epoch_owner = draw_epoch_owner(jax.random.fold_in(jax.random.fold_in(arg_keys[6], part), 71), part)
    valid_rows = draw_valid_rows(jax.random.fold_in(jax.random.fold_in(arg_keys[6], part), 71), part)
    return {"images": images, "variance": variance, "spread_kernel": spread_kernel, "shifts": shifts, "epoch_owner": epoch_owner, "valid_rows": valid_rows}


def correlate(field, kernel):
    half = KSIZE // 2
    padded = jnp.pad(field, half)
    summed = jnp.zeros_like(field)
    for row_off in range(KSIZE):
        for col_off in range(KSIZE):
            summed = summed + kernel[row_off, col_off] * padded[row_off:row_off + ROWS, col_off:col_off + COLS]
    return summed

def reference(images, variance, spread_kernel, shifts, epoch_owner, valid_rows):
    kernel_norm = spread_kernel / jnp.sum(spread_kernel)
    kernel_sq = kernel_norm * kernel_norm
    floor = 0.5 * jnp.sum(kernel_sq)
    row_ids = jnp.arange(ROWS, dtype=jnp.int32)[:, None]
    stacked = []
    for epoch in range(EPOCHS):
        slot = epoch_owner[epoch]
        exposure = images[slot]
        noise_var = variance[slot]
        usable = (row_ids >= valid_rows[epoch, 0]) & (row_ids < valid_rows[epoch, 1])
        weighted = jnp.where(usable, exposure / noise_var, jnp.float32(0.0))
        inverse = jnp.where(usable, 1.0 / noise_var, jnp.float32(0.0))
        pair = jnp.stack([correlate(weighted, kernel_norm), correlate(inverse, kernel_sq)])
        stacked.append(jnp.pad(pair, ((0, 0), (MAXS, MAXS), (MAXS, MAXS))))
    padded_all = jnp.stack(stacked)

    def one_velocity(shift):
        summed = jnp.zeros((2, ROWS, COLS), jnp.float32)
        for epoch in range(EPOCHS):
            start_row = (MAXS + shift[epoch, 0]).astype(jnp.int32)
            start_col = (MAXS + shift[epoch, 1]).astype(jnp.int32)
            summed = summed + lax.dynamic_slice(padded_all[epoch], (jnp.int32(0), start_row, start_col), (2, ROWS, COLS))
        return summed[0] / jnp.sqrt(jnp.maximum(summed[1], floor))
    return lax.map(one_velocity, shifts)
```

```python
import functools

import jax
import jax.numpy as jnp
from jax import lax
from jax.experimental import pallas as pl
from jax.experimental.pallas import tpu as pltpu
from jax.sharding import PartitionSpec as P

MAXS = 16
EPOCHS = 3
LANES = 128
SIDE = 16
LAG = 2
MESH = pl.DeviceIdType.MESH


def split(value):
    high = value.astype(jnp.bfloat16)
    return high, (value - high.astype(jnp.float32)).astype(jnp.bfloat16)


def lanes_of(shape):
    return lax.broadcasted_iota(jnp.int32, shape, len(shape) - 1)


def search_kernel(
    ksize, owner_ref, valid_ref, taps_ref, image_ref, variance_ref,
    own_ref, other_ref,
    rows_buf, left, sides, weight, acc, mine, near, up_in, up_out, down_in, down_out, final,
    halo_send, halo_recv, pre_send, pre_recv, up_send, up_recv, down_send, down_recv,
    post_send, post_recv, core_send, core_recv, keep_sem,
):
    count = lax.axis_size("vel")
    levels = count // 2
    me, core = lax.axis_index("vel"), lax.axis_index("rows")
    level, column = me // 2, me % 2
    peer = {"vel": 2 * level + 1 - column}
    above = {"vel": jnp.minimum(me + 2, count - 1)}
    below = {"vel": jnp.maximum(me - 2, 0)}
    twin = {"rows": 1 - core}
    half = ksize // 2
    blocks = rows_buf.shape[2]
    groups = LANES // blocks
    band = image_ref.shape[0] // blocks
    per = band // groups
    pairs = band // 2
    chunks = 2 * per
    halves = chunks // 2
    units = halves * EPOCHS

    barrier = pltpu.get_barrier_semaphore()

    def greet(target):
        pl.semaphore_signal(barrier, inc=1, device_id=target, device_id_type=MESH)

    greet(peer)
    greet(twin)

    @pl.when(level > 0)
    def _():
        greet(below)

    @pl.when(level < levels - 1)
    def _():
        greet(above)

    lower = jnp.int32(0)
    upper = jnp.int32(0)
    holds, close, over = [], [], []
    for e in range(EPOCHS):
        owner = owner_ref[e]
        lower += jnp.where(owner == me, valid_ref[2 * e], 0)
        upper += jnp.where(owner == me, valid_ref[2 * e + 1], 0)
        holds.append(owner == me)
        close.append(owner // 2 == level)
        over.append(owner // 2 > level)

    def fill(y, carry):
        place = pl.ds((y // per) * (blocks * per) + y % per, blocks, stride=per)
        row = core * band + y
        usable = (row >= lower) & (row < upper)
        noise = 1.0 / variance_ref[place, :]
        rows_buf[0, half + y] = jnp.where(usable, image_ref[place, :] * noise, 0.0)
        rows_buf[1, half + y] = jnp.where(usable, noise, 0.0)
        return carry

    edge = (1 - core) * (band - half)
    lax.fori_loop(edge, edge + half, fill, 0)

    @pl.when((level > 0) & (level < levels - 1))
    def _():
        pl.semaphore_wait(barrier, 4)

    @pl.when((level == 0) | (level == levels - 1))
    def _():
        pl.semaphore_wait(barrier, 3)

    halo = []
    for f in range(2):
        copy = pltpu.make_async_remote_copy(
            src_ref=rows_buf.at[f, pl.ds(half + edge, half)],
            dst_ref=rows_buf.at[f, pl.ds(core * (half + band), half)],
            send_sem=halo_send.at[f],
            recv_sem=halo_recv.at[f],
            device_id=twin,
            device_id_type=MESH,
        )
        copy.start()
        halo.append(copy)
    lax.fori_loop(core * half, core * half + band - half, fill, 0)
    empty = jnp.zeros((half, blocks, LANES), jnp.float32)
    for f in range(2):
        rows_buf[f, pl.ds(core * (half + band), half)] = empty
        rows_buf[f, 2 * half + band :] = jnp.zeros((2, blocks, LANES), jnp.float32)

    taps = taps_ref[...]
    norm = taps / jnp.sum(taps)
    row_at = lax.broadcasted_iota(jnp.int32, (LANES, LANES), 0)
    lane_at = lanes_of((LANES, LANES))
    inside = jnp.abs(row_at - lane_at) < LANES // 2
    left_in = lanes_of((SIDE, LANES)) < LANES // 2
    tiles = (ksize + 1) // 2
    window = 2 * LANES

    def put(f, tile, row, half_at, value):
        size = value.shape[0]
        high, low = split(value)
        columns = slice(half_at * LANES, (half_at + 1) * LANES)
        weight[f, tile, row : row + size, columns] = high
        weight[f, tile, window + row : window + row + size, columns] = high
        weight[f, tile, 2 * window + row : 2 * window + row + size, columns] = low

    for f in range(2):
        values = norm if f == 0 else norm * norm
        for a in range(ksize + 1 + (-(ksize + 1)) % 8):
            for p in range(2):
                if a - p < 0 or a - p >= ksize:
                    if a <= ksize:
                        put(f, a // 2, (a % 2) * LANES, p, jnp.zeros((LANES, LANES), jnp.float32))
                    put(f, tiles + a // 8, (a % 8) * 2 * SIDE, p, jnp.zeros((2 * SIDE, LANES), jnp.float32))
        for a in range(ksize):
            base = jnp.broadcast_to(values[a : a + 1, :], (8, LANES))
            base = pltpu.roll(base, 0, 1, stride=1, stride_axis=0)
            ring = jnp.concatenate([base if g == 0 else pltpu.roll(base, 8 * g, 1) for g in range(LANES // 8)], axis=0)
            own = jnp.where(inside, ring, 0.0)
            side = jnp.concatenate(
                [
                    jnp.where(left_in, ring[LANES - SIDE :], 0.0),
                    jnp.where(left_in, 0.0, ring[:SIDE]),
                ],
                axis=0,
            )
            for p in range(2):
                at = a + p
                put(f, at // 2, (at % 2) * LANES, p, own)
                put(f, tiles + at // 8, (at % 8) * 2 * SIDE, p, side)

    lane = lanes_of((blocks, LANES))
    block_at = lax.broadcasted_iota(jnp.int32, (blocks, LANES), 0)

    def beside(value):
        before = jnp.where(block_at == 0, 0.0, pltpu.roll(value, 1, 0))
        after = jnp.where(block_at == blocks - 1, 0.0, pltpu.roll(value, blocks - 1, 0))
        return jnp.where(lane >= LANES - SIDE, before, jnp.where(lane < SIDE, after, 0.0))

    def gathered(f, m):
        first = pltpu.roll(beside(rows_buf[f, 2 * m]), SIDE, 1)
        second = pltpu.roll(beside(rows_buf[f, 2 * m + 1]), 3 * SIDE, 1)
        return first + second

    def store(ref, f, m, at, value):
        high, low = split(value)
        columns = slice(at * LANES, (at + 1) * LANES)
        ref[f, m, :, columns] = high
        ref[f, m, :, window + at * LANES : window + (at + 1) * LANES] = low
        ref[f, m, :, 2 * window + at * LANES : 2 * window + (at + 1) * LANES] = high

    def operands(f):
        def step(m, this):
            for p in range(2):
                store(left, f, m, p, rows_buf[f, 2 * m + p])
            following = gathered(f, m + 1)
            both = this + pltpu.roll(following, LANES // 2, 1)
            store(sides, f, m + 2, 0, both)
            store(sides, f, m, 1, both)
            return following

        lax.fori_loop(0, half + pairs, step, gathered(f, 0))

    def correlate(f):
        def value_of(ref, m):
            return ref[f, pl.ds(m, pairs)].reshape(pairs * blocks, 3 * window)

        acc[...] = jnp.dot(value_of(left, 0), weight[f, 0], preferred_element_type=jnp.float32)

        def step(j, carry):
            acc[...] += jnp.dot(value_of(left, j), weight[f, j], preferred_element_type=jnp.float32)
            return carry

        lax.fori_loop(1, tiles, step, 0)
        for g in range(weight.shape[1] - tiles):
            acc[...] += jnp.dot(
                value_of(sides, 2 + 4 * g), weight[f, tiles + g], preferred_element_type=jnp.float32
            )
        for i in range(per):
            q, p = i // 2, i % 2
            part = [
                acc[(r * (per // 2) + q) * blocks : (r * (per // 2) + q + 1) * blocks, p * LANES : (p + 1) * LANES]
                for r in range(groups)
            ]
            mine[f * per + i] = jnp.concatenate(part, axis=0).T

    def pre_copy(k):
        return pltpu.make_async_remote_copy(
            src_ref=mine.at[2 * k + 1 - column],
            dst_ref=near.at[k],
            send_sem=pre_send.at[k],
            recv_sem=pre_recv.at[k],
            device_id=peer,
            device_id_type=MESH,
        )

    for copy in halo:
        copy.wait()
    for f in range(2):
        operands(f)
        correlate(f)
        for k in range(f * per // 2, (f + 1) * per // 2):
            pre_copy(k).start()

    def hop(source, target, send, recv, to):
        def make(u):
            return pltpu.make_async_remote_copy(
                src_ref=source.at[u],
                dst_ref=target.at[u],
                send_sem=send.at[u],
                recv_sem=recv.at[u],
                device_id=to,
                device_id_type=MESH,
            )

        return make

    up_copy = hop(up_out, up_in, up_send, up_recv, above)
    down_copy = hop(down_out, down_in, down_send, down_recv, below)

    def post_copy(u):
        e, c = u % EPOCHS, 2 * (u // EPOCHS) + column
        return pltpu.make_async_remote_copy(
            src_ref=final.at[u],
            dst_ref=own_ref.at[e, c],
            send_sem=post_send.at[u],
            recv_sem=post_recv.at[u],
            device_id=peer,
            device_id_type=MESH,
        )

    def keep_copy(u):
        e, c = u % EPOCHS, 2 * (u // EPOCHS) + column
        return pltpu.make_async_copy(final.at[u], own_ref.at[e, c], keep_sem.at[u])

    def core_copy(u, relayed):
        e = u % EPOCHS
        c = 2 * (u // EPOCHS) + ((1 - column) if relayed else column)
        return pltpu.make_async_remote_copy(
            src_ref=own_ref.at[e, c] if relayed else final.at[u],
            dst_ref=other_ref.at[e, c],
            send_sem=core_send.at[e, c],
            recv_sem=core_recv.at[e, c],
            device_id=twin,
            device_id_type=MESH,
        )

    def choose(flags, e):
        value = flags[EPOCHS - 1]
        for i in range(EPOCHS - 1):
            value = jnp.where(e == i, flags[i], value)
        return value != 0

    flag = [[jnp.where(x, 1, 0) for x in flags] for flags in (holds, close, over)]
    up_off = LAG * level
    down_off = LAG * (levels - 1 - level)
    near_off = jnp.minimum(up_off, down_off)
    far_off = jnp.maximum(up_off, down_off)

    def known(u, arrived):
        k, e = u // EPOCHS, u % EPOCHS
        local_value = jnp.where(choose(flag[0], e), mine[2 * k + column], near[k])
        return jnp.where(choose(flag[1], e), local_value, arrived)

    def slot(t, carry):
        first = t - near_off

        @pl.when((first >= 0) & (first < units) & (first % EPOCHS == 0))
        def _():
            pre_copy(first // EPOCHS).wait_recv()

        u = t - up_off

        @pl.when((u >= 0) & (u < units))
        def _():
            @pl.when(level > 0)
            def _():
                up_copy(u).wait_recv()

            up_out[u] = known(u, up_in[u])

            @pl.when(level < levels - 1)
            def _():
                up_copy(u).start()

        d = t - down_off

        @pl.when((d >= 0) & (d < units))
        def _():
            @pl.when(level < levels - 1)
            def _():
                down_copy(d).wait_recv()

            @pl.when(level > 0)
            def _():
                down_out[d] = known(d, down_in[d])
                down_copy(d).start()

        w = t - far_off

        @pl.when((w >= 0) & (w < units))
        def _():
            final[w] = jnp.where(choose(flag[2], w % EPOCHS), down_in[w], up_out[w])
            post_copy(w).start()
            keep_copy(w).start()
            core_copy(w, False).start()

        x = t - far_off - LAG

        @pl.when((x >= 0) & (x < units))
        def _():
            post_copy(x).wait_recv()
            core_copy(x, True).start()

        return carry

    lax.fori_loop(0, units + LAG * levels, slot, 0)

    def finish(u, carry):
        @pl.when(level < levels - 1)
        def _():
            up_copy(u).wait_send()

        @pl.when(level > 0)
        def _():
            down_copy(u).wait_send()

        post_copy(u).wait_send()
        keep_copy(u).wait()
        core_copy(u, False).wait()
        core_copy(u, True).wait()
        return carry

    lax.fori_loop(0, units, finish, 0)
    for k in range(halves):
        pre_copy(k).wait_send()


def search(image, variance, taps, epoch_owner, valid_rows, ksize, blocks):
    band = image.shape[0] // blocks
    per = band * blocks // LANES
    half = ksize // 2
    chunks = 2 * per
    units = chunks // 2 * EPOCHS
    tiles = (ksize + 1) // 2 + -(-(ksize + 1) // 8)
    smem = pl.BlockSpec(memory_space=pltpu.SMEM)
    vmem = pl.BlockSpec(memory_space=pltpu.VMEM)
    anywhere = pl.BlockSpec(memory_space=pl.ANY)
    plane = (LANES, LANES)
    shape = jax.ShapeDtypeStruct((EPOCHS, chunks) + plane, jnp.float32)
    dma = pltpu.SemaphoreType.DMA
    depth = 6 * LANES
    return pl.pallas_call(
        functools.partial(search_kernel, ksize),
        out_shape=(shape, shape),
        in_specs=[smem, smem, vmem, vmem, vmem],
        out_specs=(anywhere, anywhere),
        scratch_shapes=[
            pltpu.VMEM((2, band + 2 * half + 2, blocks, LANES), jnp.float32),
            pltpu.VMEM((2, band // 2 + half, blocks, depth), jnp.bfloat16),
            pltpu.VMEM((2, band // 2 + half + 2, blocks, depth), jnp.bfloat16),
            pltpu.VMEM((2, tiles, depth, 2 * LANES), jnp.bfloat16),
            pltpu.VMEM((band // 2 * blocks, 2 * LANES), jnp.float32),
            pltpu.VMEM((chunks,) + plane, jnp.float32),
            pltpu.VMEM((chunks // 2,) + plane, jnp.float32),
        ]
        + [pltpu.VMEM((units,) + plane, jnp.float32)] * 5
        + [dma((2,))] * 2
        + [dma((chunks // 2,))] * 2
        + [dma((units,))] * 6
        + [dma((EPOCHS, chunks))] * 2
        + [dma((units,))],
        compiler_params=pltpu.CompilerParams(collective_id=0, has_side_effects=True),
        name="search",
    )(epoch_owner, valid_rows.reshape(-1), taps, image, variance)


def stack_kernel(blocks, shift_ref, taps_ref, own_ref, other_ref, out_ref, held, own, other, floor_ref, own_sem, other_sem):
    vel = pl.program_id(0)
    core = lax.axis_index("rows")
    per = own.shape[1] // 2
    groups = LANES // blocks

    @pl.when(vel == 0)
    def _():
        copies = []
        for e in range(EPOCHS):
            pair = (
                pltpu.make_async_copy(own_ref.at[e], own.at[e], own_sem.at[e]),
                pltpu.make_async_copy(other_ref.at[e], other.at[e], other_sem.at[e]),
            )
            for copy in pair:
                copy.start()
            copies.append(pair)
        taps = taps_ref[...]
        norm = taps / jnp.sum(taps)
        floor_ref[0] = 0.5 * jnp.sum(norm * norm)
        lane = lanes_of((LANES, LANES))
        side_block = lanes_of((MAXS, LANES)) % blocks
        at_first = core == 0

        def arrange(e, f, i):
            here = own[e, f * per + i]
            there = other[e, f * per + i]
            before = jnp.where(at_first, 0.0, there)
            after = jnp.where(at_first, there, 0.0)
            span = MAXS // per
            for p in range(2 * span + 1):
                move = (span - p) * blocks
                if move > 0:
                    value = pltpu.roll(jnp.where(lane < LANES - move, here, before), move, 1)
                elif move < 0:
                    value = pltpu.roll(jnp.where(lane < -move, after, here), LANES + move, 1)
                else:
                    value = here
                target = held.at[2 * e + f, p * per + i]
                target[MAXS : MAXS + LANES] = value
                target[:MAXS] = jnp.where(
                    side_block == 0, 0.0, pltpu.roll(value[LANES - MAXS :], 1, 1)
                )
                target[MAXS + LANES :] = jnp.where(
                    side_block == blocks - 1, 0.0, pltpu.roll(value[:MAXS], LANES - 1, 1)
                )

        for e in range(EPOCHS):
            for copy in copies[e]:
                copy.wait()
            for f in range(2):

                def step(i, carry):
                    arrange(e, f, i)
                    return carry

                lax.fori_loop(0, per, step, 0)

    floor = floor_ref[0]
    places = []
    for e in range(EPOCHS):
        dy = shift_ref[(vel * EPOCHS + e) * 2]
        dx = shift_ref[(vel * EPOCHS + e) * 2 + 1]
        places.append((MAXS + dy, MAXS + dx))
    for i in range(per):
        sums = []
        for f in range(2):
            total = None
            for e in range(EPOCHS):
                value = held[2 * e + f, places[e][0] + i, pl.ds(places[e][1], LANES), :]
                total = value if total is None else total + value
            sums.append(total)
        value = sums[0] * lax.rsqrt(jnp.maximum(sums[1], floor))
        out_ref[0, pl.ds(i, LANES, stride=per), :] = value.T


def stack(own, other, shifts, taps, blocks):
    velocities = shifts.shape[0]
    per = own.shape[1] // 2
    smem = pl.BlockSpec(memory_space=pltpu.SMEM)
    anywhere = pl.BlockSpec(memory_space=pl.ANY)
    return pl.pallas_call(
        functools.partial(stack_kernel, blocks),
        grid=(velocities,),
        out_shape=jax.ShapeDtypeStruct((velocities, LANES * per, LANES), jnp.float32),
        in_specs=[smem, pl.BlockSpec(taps.shape, lambda v: (0, 0)), anywhere, anywhere],
        out_specs=pl.BlockSpec((1, LANES * per, LANES), lambda v: (v, 0, 0)),
        scratch_shapes=[
            pltpu.VMEM((2 * EPOCHS, per + 2 * MAXS, LANES + 2 * MAXS, LANES), jnp.float32),
            pltpu.VMEM(own.shape, jnp.float32),
            pltpu.VMEM(own.shape, jnp.float32),
            pltpu.SMEM((1,), jnp.float32),
            pltpu.SemaphoreType.DMA((EPOCHS,)),
            pltpu.SemaphoreType.DMA((EPOCHS,)),
        ],
        name="stack",
    )(shifts.reshape(-1), taps, own, other)


def local(images, variance, spread_kernel, shifts, epoch_owner, valid_rows):
    band, columns = images.shape[1:]
    ksize = spread_kernel.shape[0]
    blocks = columns // LANES
    groups = LANES // blocks
    per = band // groups

    def tiled(array):
        return array.reshape(groups, per, blocks, LANES).transpose(0, 2, 1, 3).reshape(-1, LANES)

    taps = jnp.roll(
        jnp.pad(spread_kernel[:, ::-1], ((0, 0), (0, LANES - ksize))), -(ksize // 2), axis=1
    )
    own, other = search(tiled(images), tiled(variance), taps, epoch_owner, valid_rows, ksize, blocks)
    out = stack(own, other, shifts, taps, blocks)
    out = out.reshape(-1, groups, blocks, per, LANES).transpose(0, 1, 3, 2, 4)
    return out.reshape(-1, band, columns)


def solution(mesh):
    in_specs = (
        P(("fields", "vel"), "rows", None),
        P(("fields", "vel"), "rows", None),
        P(),
        P(("fields", "vel"), None, None),
        P("fields"),
        P("fields", None),
    )
    out_specs = P(("fields", "vel"), "rows", None)
    return jax.shard_map(local, mesh=mesh, in_specs=in_specs, out_specs=out_specs, check_vma=False)
```

```python
import functools

import jax
import jax.numpy as jnp
from jax import lax
from jax.experimental import pallas as pl
from jax.experimental.pallas import tpu as pltpu
from jax.sharding import PartitionSpec as P

MAXS = 16
EPOCHS = 3
LANES = 128
SIDE = 16
LAG = 3
MESH = pl.DeviceIdType.MESH


def split(value):
    high = value.astype(jnp.bfloat16)
    return high, (value - high.astype(jnp.float32)).astype(jnp.bfloat16)


def lanes_of(shape):
    return lax.broadcasted_iota(jnp.int32, shape, len(shape) - 1)


def search_kernel(
    ksize, owner_ref, valid_ref, kernel_ref, image_ref, variance_ref,
    held_ref,
    taps_ref, own_ref, other_ref, rows_buf, left, sides, weight, acc, mine, near, up_in, up_out, down_in, down_out,
    halo_send, halo_recv, pre_send, pre_recv, up_send, up_recv, down_send, down_recv,
    post_send, post_recv, core_send, core_recv,
):
    count = lax.axis_size("vel")
    levels = count // 2
    me, core = lax.axis_index("vel"), lax.axis_index("rows")
    level, column = me // 2, me % 2
    peer = {"vel": 2 * level + 1 - column}
    above = {"vel": jnp.minimum(me + 2, count - 1)}
    below = {"vel": jnp.maximum(me - 2, 0)}
    twin = {"rows": 1 - core}
    half = ksize // 2
    blocks = rows_buf.shape[2]
    groups = LANES // blocks
    band = image_ref.shape[0] // blocks
    per = band // groups
    pairs = band // 2
    chunks = 2 * per
    halves = chunks // 2
    units = halves * EPOCHS

    barrier = pltpu.get_barrier_semaphore()

    def greet(target):
        pl.semaphore_signal(barrier, inc=1, device_id=target, device_id_type=MESH)

    greet(peer)
    greet(twin)

    @pl.when(level > 0)
    def _():
        greet(below)

    @pl.when(level < levels - 1)
    def _():
        greet(above)

    lower = jnp.int32(0)
    upper = jnp.int32(0)
    holds, close, over = [], [], []
    for e in range(EPOCHS):
        owner = owner_ref[e]
        lower += jnp.where(owner == me, valid_ref[0, e], 0)
        upper += jnp.where(owner == me, valid_ref[1, e], 0)
        holds.append(owner == me)
        close.append(owner // 2 == level)
        over.append(owner // 2 > level)

    def fill(y, carry):
        place = pl.ds((y // per) * (blocks * per) + y % per, blocks, stride=per)
        row = core * band + y
        usable = (row >= lower) & (row < upper)
        noise = 1.0 / variance_ref[place, :]
        rows_buf[0, half + y] = jnp.where(usable, image_ref[place, :] * noise, 0.0)
        rows_buf[1, half + y] = jnp.where(usable, noise, 0.0)
        return carry

    edge = (1 - core) * (band - half)
    lax.fori_loop(0, half, lambda y, carry: fill(edge + y, carry), 0, unroll=5)

    @pl.when((level > 0) & (level < levels - 1))
    def _():
        pl.semaphore_wait(barrier, 4)

    @pl.when((level == 0) | (level == levels - 1))
    def _():
        pl.semaphore_wait(barrier, 3)

    halo = []
    for f in range(2):
        copy = pltpu.make_async_remote_copy(
            src_ref=rows_buf.at[f, pl.ds(half + edge, half)],
            dst_ref=rows_buf.at[f, pl.ds(core * (half + band), half)],
            send_sem=halo_send.at[f],
            recv_sem=halo_recv.at[f],
            device_id=twin,
            device_id_type=MESH,
        )
        copy.start()
        halo.append(copy)
    lax.fori_loop(0, band - half, lambda y, carry: fill(core * half + y, carry), 0, unroll=11)
    empty = jnp.zeros((half, blocks, LANES), jnp.float32)
    for f in range(2):
        rows_buf[f, pl.ds(core * (half + band), half)] = empty
        rows_buf[f, 2 * half + band :] = jnp.zeros((2, blocks, LANES), jnp.float32)

    taps_ref[...] = jnp.zeros_like(taps_ref)
    kernel = kernel_ref[...]
    taps_ref[:ksize, :ksize] = kernel / jnp.sum(kernel)
    spot = lanes_of((8, LANES))
    spot = jnp.where(spot <= half, half - spot, jnp.where(spot >= LANES - half, half + LANES - spot, LANES - 1))
    norm = jnp.concatenate(
        [
            jnp.take_along_axis(taps_ref[8 * g : 8 * g + 8, :], spot, axis=1)
            for g in range(taps_ref.shape[0] // 8)
        ],
        axis=0,
    )
    row_at = lax.broadcasted_iota(jnp.int32, (LANES, LANES), 0)
    lane_at = lanes_of((LANES, LANES))
    inside = jnp.abs(row_at - lane_at) < LANES // 2
    left_in = lanes_of((SIDE, LANES)) < LANES // 2
    tiles = (ksize + 1) // 2
    window = 2 * LANES

    def put(f, tile, row, half_at, value):
        size = value.shape[0]
        high, low = split(value)
        columns = slice(half_at * LANES, (half_at + 1) * LANES)
        weight[f, tile, row : row + size, columns] = high
        weight[f, tile, window + row : window + row + size, columns] = high
        weight[f, tile, 2 * window + row : 2 * window + row + size, columns] = low

    for f in range(2):
        values = norm if f == 0 else norm * norm
        for a in range(ksize + 1 + (-(ksize + 1)) % 8):
            for p in range(2):
                if a - p < 0 or a - p >= ksize:
                    if a <= ksize:
                        put(f, a // 2, (a % 2) * LANES, p, jnp.zeros((LANES, LANES), jnp.float32))
                    put(f, tiles + a // 8, (a % 8) * 2 * SIDE, p, jnp.zeros((2 * SIDE, LANES), jnp.float32))
        for a in range(ksize):
            base = jnp.broadcast_to(values[a : a + 1, :], (8, LANES))
            base = pltpu.roll(base, 0, 1, stride=1, stride_axis=0)
            ring = jnp.concatenate([base if g == 0 else pltpu.roll(base, 8 * g, 1) for g in range(LANES // 8)], axis=0)
            own = jnp.where(inside, ring, 0.0)
            side = jnp.concatenate(
                [
                    jnp.where(left_in, ring[LANES - SIDE :], 0.0),
                    jnp.where(left_in, 0.0, ring[:SIDE]),
                ],
                axis=0,
            )
            for p in range(2):
                at = a + p
                put(f, at // 2, (at % 2) * LANES, p, own)
                put(f, tiles + at // 8, (at % 8) * 2 * SIDE, p, side)

    lane = lanes_of((blocks, LANES))
    block_at = lax.broadcasted_iota(jnp.int32, (blocks, LANES), 0)

    def beside(value):
        before = jnp.where(block_at == 0, 0.0, pltpu.roll(value, 1, 0))
        after = jnp.where(block_at == blocks - 1, 0.0, pltpu.roll(value, blocks - 1, 0))
        return jnp.where(lane >= LANES - SIDE, before, jnp.where(lane < SIDE, after, 0.0))

    def gathered(f, m):
        first = pltpu.roll(beside(rows_buf[f, 2 * m]), SIDE, 1)
        second = pltpu.roll(beside(rows_buf[f, 2 * m + 1]), 3 * SIDE, 1)
        return first + second

    def store(ref, f, m, at, value):
        high, low = split(value)
        columns = slice(at * LANES, (at + 1) * LANES)
        ref[f, m, :, columns] = high
        ref[f, m, :, window + at * LANES : window + (at + 1) * LANES] = low
        ref[f, m, :, 2 * window + at * LANES : 2 * window + (at + 1) * LANES] = high

    def operands(f):
        def step(m, this):
            for p in range(2):
                store(left, f, m, p, rows_buf[f, 2 * m + p])
            following = gathered(f, m + 1)
            both = this + pltpu.roll(following, LANES // 2, 1)
            store(sides, f, m + 2, 0, both)
            store(sides, f, m, 1, both)
            return following

        lax.fori_loop(0, half + pairs, step, gathered(f, 0), unroll=13)

    def correlate(f, part):
        def value_of(ref, m):
            return ref[f, pl.ds(m, pairs)].reshape(pairs * blocks, 3 * window)

        middle = (tiles + 1) // 2
        if part == 0:
            acc[...] = jnp.dot(value_of(left, 0), weight[f, 0], preferred_element_type=jnp.float32)
        for j in range(1, middle) if part == 0 else range(middle, tiles):
            acc[...] += jnp.dot(value_of(left, j), weight[f, j], preferred_element_type=jnp.float32)
        if part == 0:
            return
        for g in range(weight.shape[1] - tiles):
            acc[...] += jnp.dot(
                value_of(sides, 2 + 4 * g), weight[f, tiles + g], preferred_element_type=jnp.float32
            )
        for i in range(per):
            q, p = i // 2, i % 2
            part = [
                acc[(r * (per // 2) + q) * blocks : (r * (per // 2) + q + 1) * blocks, p * LANES : (p + 1) * LANES]
                for r in range(groups)
            ]
            mine[f * per + i] = jnp.concatenate(part, axis=0).T
        for k in range(f * per // 2, (f + 1) * per // 2):
            pre_copy(k).start()

    def pre_copy(k):
        return pltpu.make_async_remote_copy(
            src_ref=mine.at[2 * k + 1 - column],
            dst_ref=near.at[k],
            send_sem=pre_send.at[k],
            recv_sem=pre_recv.at[k],
            device_id=peer,
            device_id_type=MESH,
        )

    for copy in halo:
        copy.wait()
    operands(0)
    correlate(0, 0)
    correlate(0, 1)

    def hop(source, target, send, recv, to):
        def make(u):
            return pltpu.make_async_remote_copy(
                src_ref=source.at[u],
                dst_ref=target.at[u],
                send_sem=send.at[u],
                recv_sem=recv.at[u],
                device_id=to,
                device_id_type=MESH,
            )

        return make

    up_copy = hop(up_out, up_in, up_send, up_recv, above)
    down_copy = hop(down_out, down_in, down_send, down_recv, below)

    def post_copy(u):
        e, c = u % EPOCHS, 2 * (u // EPOCHS) + column
        return pltpu.make_async_remote_copy(
            src_ref=own_ref.at[e, c],
            dst_ref=own_ref.at[e, c],
            send_sem=post_send.at[u],
            recv_sem=post_recv.at[u],
            device_id=peer,
            device_id_type=MESH,
        )

    def core_copy(u, relayed):
        e = u % EPOCHS
        c = 2 * (u // EPOCHS) + ((1 - column) if relayed else column)
        return pltpu.make_async_remote_copy(
            src_ref=own_ref.at[e, c],
            dst_ref=other_ref.at[e, c],
            send_sem=core_send.at[e, c],
            recv_sem=core_recv.at[e, c],
            device_id=twin,
            device_id_type=MESH,
        )

    def choose(flags, e):
        value = flags[EPOCHS - 1]
        for i in range(EPOCHS - 1):
            value = jnp.where(e == i, flags[i], value)
        return value != 0

    flag = [[jnp.where(x, 1, 0) for x in flags] for flags in (holds, close, over)]
    up_off = LAG * level
    down_off = LAG * (levels - 1 - level)
    near_off = jnp.minimum(up_off, down_off)
    far_off = jnp.maximum(up_off, down_off)

    def known(u, arrived):
        k, e = u // EPOCHS, u % EPOCHS
        local_value = jnp.where(choose(flag[0], e), mine[2 * k + column], near[k])
        return jnp.where(choose(flag[1], e), local_value, arrived)

    side_block = lanes_of((MAXS, LANES)) % blocks
    at_first = core == 0

    def arrange(e, c):
        here = own_ref[e, c]
        there = other_ref[e, c]
        before = jnp.where(at_first, 0.0, there)
        after = jnp.where(at_first, there, 0.0)
        span = MAXS // per
        for p in range(2 * span + 1):
            move = (span - p) * blocks
            if move > 0:
                value = pltpu.roll(jnp.where(lane_at < LANES - move, here, before), move, 1)
            elif move < 0:
                value = pltpu.roll(jnp.where(lane_at < -move, after, here), LANES + move, 1)
            else:
                value = here
            target = held_ref.at[2 * e + c // per, p * per + c % per]
            target[MAXS : MAXS + LANES] = value
            target[:MAXS] = jnp.where(side_block == 0, 0.0, pltpu.roll(value[LANES - MAXS :], 1, 1))
            target[MAXS + LANES :] = jnp.where(
                side_block == blocks - 1, 0.0, pltpu.roll(value[:MAXS], LANES - 1, 1)
            )

    def slot(t, carry):
        first = t - near_off

        @pl.when((first >= 0) & (first < units) & (first % EPOCHS == 0))
        def _():
            pre_copy(first // EPOCHS).wait_recv()

        u = t - up_off

        @pl.when((u >= 0) & (u < units))
        def _():
            @pl.when(level > 0)
            def _():
                up_copy(u).wait_recv()

            up_out[u] = known(u, up_in[u])

            @pl.when(level < levels - 1)
            def _():
                up_copy(u).start()

        d = t - down_off

        @pl.when((d >= 0) & (d < units))
        def _():
            @pl.when(level < levels - 1)
            def _():
                down_copy(d).wait_recv()

            @pl.when(level > 0)
            def _():
                down_out[d] = known(d, down_in[d])
                down_copy(d).start()

        w = t - far_off

        @pl.when((w >= 0) & (w < units))
        def _():
            own_ref[w % EPOCHS, 2 * (w // EPOCHS) + column] = jnp.where(
                choose(flag[2], w % EPOCHS), down_in[w], up_out[w]
            )
            post_copy(w).start()
            core_copy(w, False).start()

        x = t - far_off - LAG

        @pl.when((x >= 0) & (x < units))
        def _():
            post_copy(x).wait_recv()
            core_copy(x, True).start()

        def settle(n, relayed):
            @pl.when((n >= 0) & (n < units))
            def _():
                core_copy(n, relayed).wait_recv()
                arrange(n % EPOCHS, 2 * (n // EPOCHS) + ((1 - column) if relayed else column))

        settle(t - far_off - LAG, False)
        settle(t - far_off - 2 * LAG, True)
        return carry

    def slots(first, last):
        lax.fori_loop(first, last, slot, 0)

    slots(0, LAG)
    operands(1)
    slots(LAG, 2 * LAG)
    correlate(1, 0)
    slots(2 * LAG, 3 * LAG)
    correlate(1, 1)
    slots(3 * LAG, units + LAG * (levels + 1))

    def finish(u, carry):
        @pl.when(level < levels - 1)
        def _():
            up_copy(u).wait_send()

        @pl.when(level > 0)
        def _():
            down_copy(u).wait_send()

        post_copy(u).wait_send()
        core_copy(u, False).wait_send()
        core_copy(u, True).wait_send()
        return carry

    lax.fori_loop(0, units, finish, 0)
    for k in range(halves):
        pre_copy(k).wait_send()


def search(image, variance, kernel, epoch_owner, valid_rows, blocks):
    ksize = kernel.shape[0]
    band = image.shape[0] // blocks
    per = band * blocks // LANES
    half = ksize // 2
    chunks = 2 * per
    units = chunks // 2 * EPOCHS
    tiles = (ksize + 1) // 2 + -(-(ksize + 1) // 8)
    smem = pl.BlockSpec(memory_space=pltpu.SMEM)
    vmem = pl.BlockSpec(memory_space=pltpu.VMEM)
    plane = (LANES, LANES)
    held = (2 * EPOCHS, per + 2 * MAXS, LANES + 2 * MAXS, LANES)
    dma = pltpu.SemaphoreType.DMA
    depth = 6 * LANES
    return pl.pallas_call(
        functools.partial(search_kernel, ksize),
        out_shape=pltpu.VMEM(held, jnp.float32),
        in_specs=[smem, smem, vmem, vmem, vmem],
        out_specs=vmem,
        scratch_shapes=[
            pltpu.VMEM((ksize + -ksize % 8, LANES), jnp.float32),
            pltpu.VMEM((EPOCHS, chunks) + plane, jnp.float32),
            pltpu.VMEM((EPOCHS, chunks) + plane, jnp.float32),
            pltpu.VMEM((2, band + 2 * half + 2, blocks, LANES), jnp.float32),
            pltpu.VMEM((2, band // 2 + half, blocks, depth), jnp.bfloat16),
            pltpu.VMEM((2, band // 2 + half + 2, blocks, depth), jnp.bfloat16),
            pltpu.VMEM((2, tiles, depth, 2 * LANES), jnp.bfloat16),
            pltpu.VMEM((band // 2 * blocks, 2 * LANES), jnp.float32),
            pltpu.VMEM((chunks,) + plane, jnp.float32),
            pltpu.VMEM((chunks // 2,) + plane, jnp.float32),
        ]
        + [pltpu.VMEM((units,) + plane, jnp.float32)] * 4
        + [dma((2,))] * 2
        + [dma((chunks // 2,))] * 2
        + [dma((units,))] * 6
        + [dma((EPOCHS, chunks))] * 2,
        compiler_params=pltpu.CompilerParams(
            collective_id=0, has_side_effects=True, vmem_limit_bytes=34 * 2**20
        ),
        name="search",
    )(epoch_owner, valid_rows.T, kernel, image, variance)


def stack_kernel(shift_ref, kernel_ref, held, out_ref, made, sem):
    velocities = out_ref.shape[0]
    per = held.shape[1] - 2 * MAXS
    slots = made.shape[0]
    kernel = kernel_ref[...]
    norm = kernel / jnp.sum(kernel)
    floor = 0.5 * jnp.sum(norm * norm)

    def copy(v):
        return pltpu.make_async_copy(made.at[v % slots], out_ref.at[v], sem.at[v % slots])

    def one(v, carry):
        @pl.when(v >= slots)
        def _():
            copy(v - slots).wait()

        places = [(MAXS + shift_ref[e, 0, v], MAXS + shift_ref[e, 1, v]) for e in range(EPOCHS)]
        target = made.at[v % slots]
        for i in range(per):
            sums = []
            for f in range(2):
                total = None
                for e in range(EPOCHS):
                    value = held[2 * e + f, places[e][0] + i, pl.ds(places[e][1], LANES), :]
                    total = value if total is None else total + value
                sums.append(total)
            value = sums[0] * lax.rsqrt(jnp.maximum(sums[1], floor))
            target[pl.ds(i, LANES, stride=per), :] = value.T
        copy(v).start()
        return carry

    lax.fori_loop(0, velocities, one, 0)
    for v in range(velocities - slots, velocities):
        copy(v).wait()


def stack(held, shifts, kernel):
    velocities = shifts.shape[0]
    per = held.shape[1] - 2 * MAXS
    smem = pl.BlockSpec(memory_space=pltpu.SMEM)
    vmem = pl.BlockSpec(memory_space=pltpu.VMEM)
    slots = min(3, velocities)
    return pl.pallas_call(
        stack_kernel,
        out_shape=jax.ShapeDtypeStruct((velocities, LANES * per, LANES), jnp.float32),
        in_specs=[smem, vmem, vmem],
        out_specs=pl.BlockSpec(memory_space=pl.ANY),
        scratch_shapes=[
            pltpu.VMEM((slots, LANES * per, LANES), jnp.float32),
            pltpu.SemaphoreType.DMA((slots,)),
        ],
        compiler_params=pltpu.CompilerParams(vmem_limit_bytes=8 * 2**20),
        name="stack",
    )(shifts.transpose(1, 2, 0), kernel, held)


def local(images, variance, spread_kernel, shifts, epoch_owner, valid_rows):
    band, columns = images.shape[1:]
    blocks = columns // LANES
    groups = LANES // blocks
    per = band // groups

    def tiled(array):
        return array.reshape(groups, per, blocks, LANES).transpose(0, 2, 1, 3).reshape(-1, LANES)

    held = search(tiled(images), tiled(variance), spread_kernel, epoch_owner, valid_rows, blocks)
    out = stack(held, shifts, spread_kernel)
    out = out.reshape(-1, groups, blocks, per, LANES).transpose(0, 1, 3, 2, 4)
    return out.reshape(-1, band, columns)


def solution(mesh):
    in_specs = (
        P(("fields", "vel"), "rows", None),
        P(("fields", "vel"), "rows", None),
        P(),
        P(("fields", "vel"), None, None),
        P("fields"),
        P("fields", None),
    )
    out_specs = P(("fields", "vel"), "rows", None)
    return jax.shard_map(local, mesh=mesh, in_specs=in_specs, out_specs=out_specs, check_vma=False)
```

```python
import functools

import jax
import jax.numpy as jnp
from jax import lax
from jax.experimental import pallas as pl
from jax.experimental.pallas import tpu as pltpu
from jax.sharding import PartitionSpec as P

MAXS = 16
EPOCHS = 3
LANES = 128
SIDE = 16
LAG = 3
POST = 8
CORE = 2
MESH = pl.DeviceIdType.MESH


def split(value):
    high = value.astype(jnp.bfloat16)
    return high, (value - high.astype(jnp.float32)).astype(jnp.bfloat16)


def lanes_of(shape):
    return lax.broadcasted_iota(jnp.int32, shape, len(shape) - 1)


def search_kernel(
    ksize, owner_in, valid_in, kernel_in, image_in, variance_in,
    held_ref,
    owner_ref, valid_ref, kernel_ref, image_ref, variance_ref, load_sem,
    taps_ref, own_ref, other_ref, rows_buf, left, sides, weight, acc, mine, near, up_in, up_out, down_in, down_out,
    halo_send, halo_recv, pre_send, pre_recv, up_send, up_recv, down_send, down_recv,
    post_send, post_recv, core_send, core_recv,
):
    count = lax.axis_size("vel")
    levels = count // 2
    me, core = lax.axis_index("vel"), lax.axis_index("rows")
    level, column = me // 2, me % 2
    peer = {"vel": 2 * level + 1 - column}
    above = {"vel": jnp.minimum(me + 2, count - 1)}
    below = {"vel": jnp.maximum(me - 2, 0)}
    twin = {"rows": 1 - core}
    half = ksize // 2
    blocks = rows_buf.shape[2]
    groups = LANES // blocks
    band = image_ref.shape[0] // blocks
    per = band // groups
    pairs = band // 2
    chunks = 2 * per
    halves = chunks // 2
    units = halves * EPOCHS

    loads = [
        pltpu.make_async_copy(source, target, load_sem.at[i])
        for i, (source, target) in enumerate(
            (
                (owner_in, owner_ref),
                (valid_in, valid_ref),
                (image_in, image_ref),
                (variance_in, variance_ref),
                (kernel_in, kernel_ref),
            )
        )
    ]
    for load in loads:
        load.start()

    barrier = pltpu.get_barrier_semaphore()

    def greet(target):
        pl.semaphore_signal(barrier, inc=1, device_id=target, device_id_type=MESH)

    greet(peer)
    greet(twin)

    @pl.when(level > 0)
    def _():
        greet(below)

    @pl.when(level < levels - 1)
    def _():
        greet(above)

    for load in loads:
        load.wait()

    lower = jnp.int32(0)
    upper = jnp.int32(0)
    holds, close, over = [], [], []
    for e in range(EPOCHS):
        owner = owner_ref[e]
        lower += jnp.where(owner == me, valid_ref[0, e], 0)
        upper += jnp.where(owner == me, valid_ref[1, e], 0)
        holds.append(owner == me)
        close.append(owner // 2 == level)
        over.append(owner // 2 > level)

    def fill(y, carry):
        place = pl.ds((y // per) * (blocks * per) + y % per, blocks, stride=per)
        row = core * band + y
        usable = (row >= lower) & (row < upper)
        noise = 1.0 / variance_ref[place, :]
        rows_buf[0, half + y] = jnp.where(usable, image_ref[place, :] * noise, 0.0)
        rows_buf[1, half + y] = jnp.where(usable, noise, 0.0)
        return carry

    edge = (1 - core) * (band - half)
    lax.fori_loop(0, half, lambda y, carry: fill(edge + y, carry), 0, unroll=5)

    @pl.when((level > 0) & (level < levels - 1))
    def _():
        pl.semaphore_wait(barrier, 4)

    @pl.when((level == 0) | (level == levels - 1))
    def _():
        pl.semaphore_wait(barrier, 3)

    halo = []
    for f in range(2):
        copy = pltpu.make_async_remote_copy(
            src_ref=rows_buf.at[f, pl.ds(half + edge, half)],
            dst_ref=rows_buf.at[f, pl.ds(core * (half + band), half)],
            send_sem=halo_send.at[f],
            recv_sem=halo_recv.at[f],
            device_id=twin,
            device_id_type=MESH,
        )
        copy.start()
        halo.append(copy)
    lax.fori_loop(0, band - half, lambda y, carry: fill(core * half + y, carry), 0, unroll=11)
    empty = jnp.zeros((half, blocks, LANES), jnp.float32)
    for f in range(2):
        rows_buf[f, pl.ds(core * (half + band), half)] = empty
        rows_buf[f, 2 * half + band :] = jnp.zeros((2, blocks, LANES), jnp.float32)

    taps_ref[...] = jnp.zeros_like(taps_ref)
    kernel = kernel_ref[...]
    taps_ref[:ksize, :ksize] = kernel / jnp.sum(kernel)
    spot = lanes_of((8, LANES))
    spot = jnp.where(spot <= half, half - spot, jnp.where(spot >= LANES - half, half + LANES - spot, LANES - 1))
    norm = jnp.concatenate(
        [
            jnp.take_along_axis(taps_ref[8 * g : 8 * g + 8, :], spot, axis=1)
            for g in range(taps_ref.shape[0] // 8)
        ],
        axis=0,
    )
    row_at = lax.broadcasted_iota(jnp.int32, (LANES, LANES), 0)
    lane_at = lanes_of((LANES, LANES))
    inside = jnp.abs(row_at - lane_at) < LANES // 2
    left_in = lanes_of((SIDE, LANES)) < LANES // 2
    tiles = (ksize + 1) // 2
    window = 2 * LANES

    def put(f, tile, row, half_at, value):
        size = value.shape[0]
        high, low = split(value)
        columns = slice(half_at * LANES, (half_at + 1) * LANES)
        weight[f, tile, row : row + size, columns] = high
        weight[f, tile, window + row : window + row + size, columns] = high
        weight[f, tile, 2 * window + row : 2 * window + row + size, columns] = low

    def weights(f, first, last):
        values = norm if f == 0 else norm * norm
        for a in range(ksize + 1 + (-(ksize + 1)) % 8):
            for p in range(2):
                if first == 0 and (a - p < 0 or a - p >= ksize):
                    if a <= ksize:
                        put(f, a // 2, (a % 2) * LANES, p, jnp.zeros((LANES, LANES), jnp.float32))
                    put(f, tiles + a // 8, (a % 8) * 2 * SIDE, p, jnp.zeros((2 * SIDE, LANES), jnp.float32))
        for a in range(first, last):
            base = jnp.broadcast_to(values[a : a + 1, :], (8, LANES))
            base = pltpu.roll(base, 0, 1, stride=1, stride_axis=0)
            ring = jnp.concatenate([base if g == 0 else pltpu.roll(base, 8 * g, 1) for g in range(LANES // 8)], axis=0)
            own = jnp.where(inside, ring, 0.0)
            side = jnp.concatenate(
                [
                    jnp.where(left_in, ring[LANES - SIDE :], 0.0),
                    jnp.where(left_in, 0.0, ring[:SIDE]),
                ],
                axis=0,
            )
            for p in range(2):
                at = a + p
                put(f, at // 2, (at % 2) * LANES, p, own)
                put(f, tiles + at // 8, (at % 8) * 2 * SIDE, p, side)

    weights(0, 0, ksize)

    lane = lanes_of((blocks, LANES))
    block_at = lax.broadcasted_iota(jnp.int32, (blocks, LANES), 0)

    def beside(value):
        before = jnp.where(block_at == 0, 0.0, pltpu.roll(value, 1, 0))
        after = jnp.where(block_at == blocks - 1, 0.0, pltpu.roll(value, blocks - 1, 0))
        return jnp.where(lane >= LANES - SIDE, before, jnp.where(lane < SIDE, after, 0.0))

    def gathered(f, m):
        first = pltpu.roll(beside(rows_buf[f, 2 * m]), SIDE, 1)
        second = pltpu.roll(beside(rows_buf[f, 2 * m + 1]), 3 * SIDE, 1)
        return first + second

    def store(ref, f, m, at, value):
        high, low = split(value)
        columns = slice(at * LANES, (at + 1) * LANES)
        ref[f, m, :, columns] = high
        ref[f, m, :, window + at * LANES : window + (at + 1) * LANES] = low
        ref[f, m, :, 2 * window + at * LANES : 2 * window + (at + 1) * LANES] = high

    def operands(f, first, last):
        def step(m, this):
            for p in range(2):
                store(left, f, m, p, rows_buf[f, 2 * m + p])
            following = gathered(f, m + 1)
            both = this + pltpu.roll(following, LANES // 2, 1)
            store(sides, f, m + 2, 0, both)
            store(sides, f, m, 1, both)
            return following

        lax.fori_loop(first, last, step, gathered(f, first), unroll=last - first)

    products = weight.shape[1]

    def correlate(f, first, last):
        for j in range(first, last):
            ref, m = (left, j) if j < tiles else (sides, 2 + 4 * (j - tiles))
            value = ref[f, pl.ds(m, pairs)].reshape(pairs * blocks, 3 * window)
            value = jnp.dot(value, weight[f, j], preferred_element_type=jnp.float32)
            if j == 0:
                acc[...] = value
            else:
                acc[...] += value
        if last < products:
            return
        for i in range(per):
            q, p = i // 2, i % 2
            part = [
                acc[(r * (per // 2) + q) * blocks : (r * (per // 2) + q + 1) * blocks, p * LANES : (p + 1) * LANES]
                for r in range(groups)
            ]
            mine[f * per + i] = jnp.concatenate(part, axis=0).T
        for k in range(f * per // 2, (f + 1) * per // 2):
            pre_copy(k).start()

    def pre_copy(k):
        return pltpu.make_async_remote_copy(
            src_ref=mine.at[2 * k + 1 - column],
            dst_ref=near.at[k],
            send_sem=pre_send.at[k],
            recv_sem=pre_recv.at[k],
            device_id=peer,
            device_id_type=MESH,
        )

    for copy in halo:
        copy.wait()
    depth = half + pairs
    operands(0, 0, depth)
    correlate(0, 0, products)

    def hop(source, target, send, recv, to):
        def make(u):
            return pltpu.make_async_remote_copy(
                src_ref=source.at[u],
                dst_ref=target.at[u],
                send_sem=send.at[u],
                recv_sem=recv.at[u],
                device_id=to,
                device_id_type=MESH,
            )

        return make

    up_copy = hop(up_out, up_in, up_send, up_recv, above)
    down_copy = hop(down_out, down_in, down_send, down_recv, below)

    def post_copy(u):
        e, c = u % EPOCHS, 2 * (u // EPOCHS) + column
        return pltpu.make_async_remote_copy(
            src_ref=own_ref.at[e, c],
            dst_ref=own_ref.at[e, c],
            send_sem=post_send.at[u],
            recv_sem=post_recv.at[u],
            device_id=peer,
            device_id_type=MESH,
        )

    def core_copy(u, relayed):
        e = u % EPOCHS
        c = 2 * (u // EPOCHS) + ((1 - column) if relayed else column)
        return pltpu.make_async_remote_copy(
            src_ref=own_ref.at[e, c],
            dst_ref=other_ref.at[e, c],
            send_sem=core_send.at[e, c],
            recv_sem=core_recv.at[e, c],
            device_id=twin,
            device_id_type=MESH,
        )

    def choose(flags, e):
        value = flags[EPOCHS - 1]
        for i in range(EPOCHS - 1):
            value = jnp.where(e == i, flags[i], value)
        return value != 0

    flag = [[jnp.where(x, 1, 0) for x in flags] for flags in (holds, close, over)]
    up_off = LAG * level
    down_off = LAG * (levels - 1 - level)
    near_off = jnp.minimum(up_off, down_off)
    far_off = jnp.maximum(up_off, down_off)

    def known(u, arrived):
        k, e = u // EPOCHS, u % EPOCHS
        local_value = jnp.where(choose(flag[0], e), mine[2 * k + column], near[k])
        return jnp.where(choose(flag[1], e), local_value, arrived)

    side_block = lanes_of((MAXS, LANES)) % blocks
    at_first = core == 0

    def arrange(e, c):
        here = own_ref[e, c]
        there = other_ref[e, c]
        before = jnp.where(at_first, 0.0, there)
        after = jnp.where(at_first, there, 0.0)
        span = MAXS // per
        for p in range(2 * span + 1):
            move = (span - p) * blocks
            if move > 0:
                value = pltpu.roll(jnp.where(lane_at < LANES - move, here, before), move, 1)
            elif move < 0:
                value = pltpu.roll(jnp.where(lane_at < -move, after, here), LANES + move, 1)
            else:
                value = here
            target = held_ref.at[2 * e + c // per, p * per + c % per]
            target[MAXS : MAXS + LANES] = value
            target[:MAXS] = jnp.where(side_block == 0, 0.0, pltpu.roll(value[LANES - MAXS :], 1, 1))
            target[MAXS + LANES :] = jnp.where(
                side_block == blocks - 1, 0.0, pltpu.roll(value[:MAXS], LANES - 1, 1)
            )

    def slot(t, carry):
        first = t - near_off

        @pl.when((first >= 0) & (first < units) & (first % EPOCHS == 0))
        def _():
            pre_copy(first // EPOCHS).wait_recv()

        u = t - up_off

        @pl.when((u >= 0) & (u < units))
        def _():
            @pl.when(level > 0)
            def _():
                up_copy(u).wait_recv()

            up_out[u] = known(u, up_in[u])

            @pl.when(level < levels - 1)
            def _():
                up_copy(u).start()

        d = t - down_off

        @pl.when((d >= 0) & (d < units))
        def _():
            @pl.when(level < levels - 1)
            def _():
                down_copy(d).wait_recv()

            @pl.when(level > 0)
            def _():
                down_out[d] = known(d, down_in[d])
                down_copy(d).start()

        w = t - far_off

        @pl.when((w >= 0) & (w < units))
        def _():
            own_ref[w % EPOCHS, 2 * (w // EPOCHS) + column] = jnp.where(
                choose(flag[2], w % EPOCHS), down_in[w], up_out[w]
            )
            post_copy(w).start()
            core_copy(w, False).start()

        x = t - far_off - POST

        @pl.when((x >= 0) & (x < units))
        def _():
            post_copy(x).wait_recv()
            core_copy(x, True).start()

        def settle(n, relayed):
            @pl.when((n >= 0) & (n < units))
            def _():
                core_copy(n, relayed).wait_recv()
                arrange(n % EPOCHS, 2 * (n // EPOCHS) + ((1 - column) if relayed else column))

        settle(t - far_off - CORE, False)
        settle(t - far_off - POST - CORE, True)
        return carry

    def slots(first, last):
        lax.fori_loop(first, last, slot, 0)

    pieces = [
        functools.partial(weights, 1, 0, ksize // 2),
        functools.partial(weights, 1, ksize // 2, ksize),
        functools.partial(operands, 1, 0, depth // 2),
        functools.partial(operands, 1, depth // 2, depth),
    ]
    cuts = [products * i // 4 for i in range(5)]
    pieces += [functools.partial(correlate, 1, cuts[i], cuts[i + 1]) for i in range(4)]
    for t, piece in enumerate(pieces):
        slots(t, t + 1)
        piece()
    slots(len(pieces), units + LAG * (levels - 1) + POST + CORE)

    def finish(u, carry):
        @pl.when(level < levels - 1)
        def _():
            up_copy(u).wait_send()

        @pl.when(level > 0)
        def _():
            down_copy(u).wait_send()

        post_copy(u).wait_send()
        core_copy(u, False).wait_send()
        core_copy(u, True).wait_send()
        return carry

    lax.fori_loop(0, units, finish, 0)
    for k in range(halves):
        pre_copy(k).wait_send()


def search(image, variance, kernel, epoch_owner, valid_rows, blocks):
    ksize = kernel.shape[0]
    band = image.shape[0] // blocks
    per = band * blocks // LANES
    half = ksize // 2
    chunks = 2 * per
    units = chunks // 2 * EPOCHS
    tiles = (ksize + 1) // 2 + -(-(ksize + 1) // 8)
    vmem = pl.BlockSpec(memory_space=pltpu.VMEM)
    plane = (LANES, LANES)
    held = (2 * EPOCHS, per + 2 * MAXS, LANES + 2 * MAXS, LANES)
    dma = pltpu.SemaphoreType.DMA
    depth = 6 * LANES
    return pl.pallas_call(
        functools.partial(search_kernel, ksize),
        out_shape=pltpu.VMEM(held, jnp.float32),
        in_specs=[pl.BlockSpec(memory_space=pltpu.HBM)] * 5,
        out_specs=vmem,
        scratch_shapes=[
            pltpu.SMEM(epoch_owner.shape, jnp.int32),
            pltpu.SMEM(valid_rows.shape[::-1], jnp.int32),
            pltpu.VMEM(kernel.shape, jnp.float32),
            pltpu.VMEM(image.shape, jnp.float32),
            pltpu.VMEM(image.shape, jnp.float32),
            dma((5,)),
            pltpu.VMEM((ksize + -ksize % 8, LANES), jnp.float32),
            pltpu.VMEM((EPOCHS, chunks) + plane, jnp.float32),
            pltpu.VMEM((EPOCHS, chunks) + plane, jnp.float32),
            pltpu.VMEM((2, band + 2 * half + 2, blocks, LANES), jnp.float32),
            pltpu.VMEM((2, band // 2 + half, blocks, depth), jnp.bfloat16),
            pltpu.VMEM((2, band // 2 + half + 2, blocks, depth), jnp.bfloat16),
            pltpu.VMEM((2, tiles, depth, 2 * LANES), jnp.bfloat16),
            pltpu.VMEM((band // 2 * blocks, 2 * LANES), jnp.float32),
            pltpu.VMEM((chunks,) + plane, jnp.float32),
            pltpu.VMEM((chunks // 2,) + plane, jnp.float32),
        ]
        + [pltpu.VMEM((units,) + plane, jnp.float32)] * 4
        + [dma((2,))] * 2
        + [dma((chunks // 2,))] * 2
        + [dma((units,))] * 6
        + [dma((EPOCHS, chunks))] * 2,
        compiler_params=pltpu.CompilerParams(
            collective_id=0, has_side_effects=True, vmem_limit_bytes=34 * 2**20
        ),
        name="search",
    )(*[
        pltpu.with_memory_space_constraint(x, pltpu.HBM)
        for x in (epoch_owner, valid_rows.T, kernel, image, variance)
    ])


def stack_kernel(shift_ref, kernel_ref, held, out_ref, made, sem):
    velocities = out_ref.shape[0]
    per = held.shape[1] - 2 * MAXS
    slots = made.shape[0]
    kernel = kernel_ref[...]
    norm = kernel / jnp.sum(kernel)
    floor = 0.5 * jnp.sum(norm * norm)

    def copy(v):
        return pltpu.make_async_copy(made.at[v % slots], out_ref.at[v], sem.at[v % slots])

    def one(v, carry):
        @pl.when(v >= slots)
        def _():
            copy(v - slots).wait()

        places = [(MAXS + shift_ref[e, 0, v], MAXS + shift_ref[e, 1, v]) for e in range(EPOCHS)]
        target = made.at[v % slots]
        for i in range(per):
            sums = []
            for f in range(2):
                total = None
                for e in range(EPOCHS):
                    value = held[2 * e + f, places[e][0] + i, pl.ds(places[e][1], LANES), :]
                    total = value if total is None else total + value
                sums.append(total)
            value = sums[0] * lax.rsqrt(jnp.maximum(sums[1], floor))
            target[pl.ds(i, LANES, stride=per), :] = value.T
        copy(v).start()
        return carry

    lax.fori_loop(0, velocities, one, 0)
    for v in range(velocities - slots, velocities):
        copy(v).wait()


def stack(held, shifts, kernel):
    velocities = shifts.shape[0]
    per = held.shape[1] - 2 * MAXS
    smem = pl.BlockSpec(memory_space=pltpu.SMEM)
    vmem = pl.BlockSpec(memory_space=pltpu.VMEM)
    slots = min(3, velocities)
    return pl.pallas_call(
        stack_kernel,
        out_shape=jax.ShapeDtypeStruct((velocities, LANES * per, LANES), jnp.float32),
        in_specs=[smem, vmem, vmem],
        out_specs=pl.BlockSpec(memory_space=pl.ANY),
        scratch_shapes=[
            pltpu.VMEM((slots, LANES * per, LANES), jnp.float32),
            pltpu.SemaphoreType.DMA((slots,)),
        ],
        compiler_params=pltpu.CompilerParams(vmem_limit_bytes=8 * 2**20),
        name="stack",
    )(shifts.transpose(1, 2, 0), kernel, held)


def local(images, variance, spread_kernel, shifts, epoch_owner, valid_rows):
    band, columns = images.shape[1:]
    blocks = columns // LANES
    groups = LANES // blocks
    per = band // groups

    def tiled(array):
        return array.reshape(groups, per, blocks, LANES).transpose(0, 2, 1, 3).reshape(-1, LANES)

    held = search(tiled(images), tiled(variance), spread_kernel, epoch_owner, valid_rows, blocks)
    out = stack(held, shifts, spread_kernel)
    out = out.reshape(-1, groups, blocks, per, LANES).transpose(0, 1, 3, 2, 4)
    return out.reshape(-1, band, columns)


def solution(mesh):
    in_specs = (
        P(("fields", "vel"), "rows", None),
        P(("fields", "vel"), "rows", None),
        P(),
        P(("fields", "vel"), None, None),
        P("fields"),
        P("fields", None),
    )
    out_specs = P(("fields", "vel"), "rows", None)
    return jax.shard_map(local, mesh=mesh, in_specs=in_specs, out_specs=out_specs, check_vma=False)
```

```python
import functools

import jax
import jax.numpy as jnp
from jax import lax
from jax.experimental import pallas as pl
from jax.experimental.pallas import tpu as pltpu
from jax.sharding import PartitionSpec as P

MAXS = 16
EPOCHS = 3
LANES = 128
SIDE = 16
LAG = 3
POST = 8
CORE = 2
MESH = pl.DeviceIdType.MESH


def split(value):
    high = value.astype(jnp.bfloat16)
    return high, (value - high.astype(jnp.float32)).astype(jnp.bfloat16)


def lanes_of(shape):
    return lax.broadcasted_iota(jnp.int32, shape, len(shape) - 1)


def search_kernel(
    ksize, owner_in, valid_in, kernel_in, image_in, variance_in,
    held_ref,
    owner_ref, valid_ref, kernel_ref, image_ref, variance_ref, load_sem,
    taps_ref, own_ref, other_ref, rows_buf, left, sides, weight, acc, mine, near, up_in, up_out, down_in, down_out,
    halo_send, halo_recv, pre_send, pre_recv, up_send, up_recv, down_send, down_recv,
    post_send, post_recv, core_send, core_recv,
):
    count = lax.axis_size("vel")
    levels = count // 2
    me, core = lax.axis_index("vel"), lax.axis_index("rows")
    level, column = me // 2, me % 2
    peer = {"vel": 2 * level + 1 - column}
    above = {"vel": jnp.minimum(me + 2, count - 1)}
    below = {"vel": jnp.maximum(me - 2, 0)}
    twin = {"rows": 1 - core}
    half = ksize // 2
    blocks = rows_buf.shape[2]
    groups = LANES // blocks
    band = image_ref.shape[0] // blocks
    per = band // groups
    pairs = band // 2
    chunks = 2 * per
    halves = chunks // 2
    units = halves * EPOCHS

    loads = [
        pltpu.make_async_copy(source, target, load_sem.at[i])
        for i, (source, target) in enumerate(
            (
                (owner_in, owner_ref),
                (valid_in, valid_ref),
                (image_in, image_ref),
                (variance_in, variance_ref),
                (kernel_in, kernel_ref),
            )
        )
    ]
    for load in loads:
        load.start()

    barrier = pltpu.get_barrier_semaphore()

    def greet(target):
        pl.semaphore_signal(barrier, inc=1, device_id=target, device_id_type=MESH)

    greet(peer)
    greet(twin)

    @pl.when(level > 0)
    def _():
        greet(below)

    @pl.when(level < levels - 1)
    def _():
        greet(above)

    for load in loads:
        load.wait()

    lower = jnp.int32(0)
    upper = jnp.int32(0)
    holds, close, over = [], [], []
    for e in range(EPOCHS):
        owner = owner_ref[e]
        lower += jnp.where(owner == me, valid_ref[0, e], 0)
        upper += jnp.where(owner == me, valid_ref[1, e], 0)
        holds.append(owner == me)
        close.append(owner // 2 == level)
        over.append(owner // 2 > level)

    def fill(y, carry):
        place = pl.ds((y // per) * (blocks * per) + y % per, blocks, stride=per)
        row = core * band + y
        usable = (row >= lower) & (row < upper)
        noise = 1.0 / variance_ref[place, :]
        rows_buf[0, half + y] = jnp.where(usable, image_ref[place, :] * noise, 0.0)
        rows_buf[1, half + y] = jnp.where(usable, noise, 0.0)
        return carry

    edge = (1 - core) * (band - half)
    lax.fori_loop(0, half, lambda y, carry: fill(edge + y, carry), 0, unroll=5)

    @pl.when((level > 0) & (level < levels - 1))
    def _():
        pl.semaphore_wait(barrier, 4)

    @pl.when((level == 0) | (level == levels - 1))
    def _():
        pl.semaphore_wait(barrier, 3)

    halo = []
    for f in range(2):
        copy = pltpu.make_async_remote_copy(
            src_ref=rows_buf.at[f, pl.ds(half + edge, half)],
            dst_ref=rows_buf.at[f, pl.ds(core * (half + band), half)],
            send_sem=halo_send.at[f],
            recv_sem=halo_recv.at[f],
            device_id=twin,
            device_id_type=MESH,
        )
        copy.start()
        halo.append(copy)
    lax.fori_loop(0, band - half, lambda y, carry: fill(core * half + y, carry), 0, unroll=11)
    empty = jnp.zeros((half, blocks, LANES), jnp.float32)
    for f in range(2):
        rows_buf[f, pl.ds(core * (half + band), half)] = empty
        rows_buf[f, 2 * half + band :] = jnp.zeros((2, blocks, LANES), jnp.float32)

    taps_ref[...] = jnp.zeros_like(taps_ref)
    kernel = kernel_ref[...]
    taps_ref[:ksize, :ksize] = kernel / jnp.sum(kernel)
    spot = lanes_of((8, LANES))
    spot = jnp.where(spot <= half, half - spot, jnp.where(spot >= LANES - half, half + LANES - spot, LANES - 1))
    norm = jnp.concatenate(
        [
            jnp.take_along_axis(taps_ref[8 * g : 8 * g + 8, :], spot, axis=1)
            for g in range(taps_ref.shape[0] // 8)
        ],
        axis=0,
    )
    row_at = lax.broadcasted_iota(jnp.int32, (LANES, LANES), 0)
    lane_at = lanes_of((LANES, LANES))
    inside = jnp.abs(row_at - lane_at) < LANES // 2
    left_in = lanes_of((SIDE, LANES)) < LANES // 2
    tiles = (ksize + 1) // 2
    window = 2 * LANES

    def put(f, tile, row, half_at, value):
        size = value.shape[0]
        high, low = split(value)
        columns = slice(half_at * LANES, (half_at + 1) * LANES)
        weight[f, tile, row : row + size, columns] = high
        weight[f, tile, window + row : window + row + size, columns] = high
        weight[f, tile, 2 * window + row : 2 * window + row + size, columns] = low

    def weights(f, first, last):
        values = norm if f == 0 else norm * norm
        for a in range(ksize + 1 + (-(ksize + 1)) % 8):
            for p in range(2):
                if first == 0 and (a - p < 0 or a - p >= ksize):
                    if a <= ksize:
                        put(f, a // 2, (a % 2) * LANES, p, jnp.zeros((LANES, LANES), jnp.float32))
                    put(f, tiles + a // 8, (a % 8) * 2 * SIDE, p, jnp.zeros((2 * SIDE, LANES), jnp.float32))
        for a in range(first, last):
            base = jnp.broadcast_to(values[a : a + 1, :], (8, LANES))
            base = pltpu.roll(base, 0, 1, stride=1, stride_axis=0)
            ring = jnp.concatenate([base if g == 0 else pltpu.roll(base, 8 * g, 1) for g in range(LANES // 8)], axis=0)
            own = jnp.where(inside, ring, 0.0)
            side = jnp.concatenate(
                [
                    jnp.where(left_in, ring[LANES - SIDE :], 0.0),
                    jnp.where(left_in, 0.0, ring[:SIDE]),
                ],
                axis=0,
            )
            for p in range(2):
                at = a + p
                put(f, at // 2, (at % 2) * LANES, p, own)
                put(f, tiles + at // 8, (at % 8) * 2 * SIDE, p, side)

    weights(0, 0, ksize)

    lane = lanes_of((blocks, LANES))
    block_at = lax.broadcasted_iota(jnp.int32, (blocks, LANES), 0)

    def beside(value):
        before = jnp.where(block_at == 0, 0.0, pltpu.roll(value, 1, 0))
        after = jnp.where(block_at == blocks - 1, 0.0, pltpu.roll(value, blocks - 1, 0))
        return jnp.where(lane >= LANES - SIDE, before, jnp.where(lane < SIDE, after, 0.0))

    def gathered(f, m):
        first = pltpu.roll(beside(rows_buf[f, 2 * m]), SIDE, 1)
        second = pltpu.roll(beside(rows_buf[f, 2 * m + 1]), 3 * SIDE, 1)
        return first + second

    def store(ref, f, m, at, value):
        high, low = split(value)
        columns = slice(at * LANES, (at + 1) * LANES)
        ref[f, m, :, columns] = high
        ref[f, m, :, window + at * LANES : window + (at + 1) * LANES] = low
        ref[f, m, :, 2 * window + at * LANES : 2 * window + (at + 1) * LANES] = high

    def operands(f, first, last, base=0):
        def step(m, this):
            for p in range(2):
                store(left, f, m, p, rows_buf[f, 2 * m + p])
            following = gathered(f, m + 1)
            both = this + pltpu.roll(following, LANES // 2, 1)
            store(sides, f, m + 2, 0, both)
            store(sides, f, m, 1, both)
            return following

        start = gathered(f, base + first)
        lax.fori_loop(first, last, lambda m, carry: step(base + m, carry), start, unroll=last - first)

    products = weight.shape[1]

    def product(f, ref, m, j):
        value = ref[f, pl.ds(m, pairs)].reshape(pairs * blocks, 3 * window)
        return jnp.dot(value, weight[f, j], preferred_element_type=jnp.float32)

    def correlate(f, first, last):
        for j in range(first, last):
            value = product(f, left, j, j) if j < tiles else product(f, sides, 2 + 4 * (j - tiles), j)
            if j == 0:
                acc[...] = value
            else:
                acc[...] += value
        if last < products:
            return
        for i in range(per):
            q, p = i // 2, i % 2
            part = [
                acc[(r * (per // 2) + q) * blocks : (r * (per // 2) + q + 1) * blocks, p * LANES : (p + 1) * LANES]
                for r in range(groups)
            ]
            mine[f * per + i] = jnp.concatenate(part, axis=0).T
        for k in range(f * per // 2, (f + 1) * per // 2):
            pre_copy(k).start()

    def pre_copy(k):
        return pltpu.make_async_remote_copy(
            src_ref=mine.at[2 * k + 1 - column],
            dst_ref=near.at[k],
            send_sem=pre_send.at[k],
            recv_sem=pre_recv.at[k],
            device_id=peer,
            device_id_type=MESH,
        )

    depth = half + pairs
    alone = depth - half // 2 - 1
    operands(0, 0, alone, core * (depth - alone))
    ready = alone - pairs + 1
    first = core * (tiles - ready)
    acc[...] = product(0, left, first, first)
    for i in range(1, ready):
        acc[...] += product(0, left, first + i, first + i)
    for copy in halo:
        copy.wait()
    operands(0, 0, depth - alone, (1 - core) * alone)
    first = (1 - core) * ready
    for i in range(tiles - ready):
        acc[...] += product(0, left, first + i, first + i)
    correlate(0, tiles, products)

    def hop(source, target, send, recv, to):
        def make(u):
            return pltpu.make_async_remote_copy(
                src_ref=source.at[u],
                dst_ref=target.at[u],
                send_sem=send.at[u],
                recv_sem=recv.at[u],
                device_id=to,
                device_id_type=MESH,
            )

        return make

    up_copy = hop(up_out, up_in, up_send, up_recv, above)
    down_copy = hop(down_out, down_in, down_send, down_recv, below)

    def post_copy(u):
        e, c = u % EPOCHS, 2 * (u // EPOCHS) + column
        return pltpu.make_async_remote_copy(
            src_ref=own_ref.at[e, c],
            dst_ref=own_ref.at[e, c],
            send_sem=post_send.at[u],
            recv_sem=post_recv.at[u],
            device_id=peer,
            device_id_type=MESH,
        )

    def core_copy(u, relayed):
        e = u % EPOCHS
        c = 2 * (u // EPOCHS) + ((1 - column) if relayed else column)
        return pltpu.make_async_remote_copy(
            src_ref=own_ref.at[e, c],
            dst_ref=other_ref.at[e, c],
            send_sem=core_send.at[e, c],
            recv_sem=core_recv.at[e, c],
            device_id=twin,
            device_id_type=MESH,
        )

    def choose(flags, e):
        value = flags[EPOCHS - 1]
        for i in range(EPOCHS - 1):
            value = jnp.where(e == i, flags[i], value)
        return value != 0

    flag = [[jnp.where(x, 1, 0) for x in flags] for flags in (holds, close, over)]
    up_off = LAG * level
    down_off = LAG * (levels - 1 - level)
    near_off = jnp.minimum(up_off, down_off)
    far_off = jnp.maximum(up_off, down_off)

    def known(u, arrived):
        k, e = u // EPOCHS, u % EPOCHS
        local_value = jnp.where(choose(flag[0], e), mine[2 * k + column], near[k])
        return jnp.where(choose(flag[1], e), local_value, arrived)

    side_block = lanes_of((MAXS, LANES)) % blocks
    at_first = core == 0

    def arrange(e, c):
        here = own_ref[e, c]
        there = other_ref[e, c]
        before = jnp.where(at_first, 0.0, there)
        after = jnp.where(at_first, there, 0.0)
        span = MAXS // per
        for p in range(2 * span + 1):
            move = (span - p) * blocks
            if move > 0:
                value = pltpu.roll(jnp.where(lane_at < LANES - move, here, before), move, 1)
            elif move < 0:
                value = pltpu.roll(jnp.where(lane_at < -move, after, here), LANES + move, 1)
            else:
                value = here
            target = held_ref.at[2 * e + c // per, p * per + c % per]
            target[MAXS : MAXS + LANES] = value
            target[:MAXS] = jnp.where(side_block == 0, 0.0, pltpu.roll(value[LANES - MAXS :], 1, 1))
            target[MAXS + LANES :] = jnp.where(
                side_block == blocks - 1, 0.0, pltpu.roll(value[:MAXS], LANES - 1, 1)
            )

    def slot(t, carry):
        first = t - near_off

        @pl.when((first >= 0) & (first < units) & (first % EPOCHS == 0))
        def _():
            pre_copy(first // EPOCHS).wait_recv()

        u = t - up_off

        def upward():
            @pl.when(level > 0)
            def _():
                up_copy(u).wait_recv()

            up_out[u] = known(u, up_in[u])

            @pl.when(level < levels - 1)
            def _():
                up_copy(u).start()

        d = t - down_off

        def downward():
            @pl.when(level < levels - 1)
            def _():
                down_copy(d).wait_recv()

            @pl.when(level > 0)
            def _():
                down_out[d] = known(d, down_in[d])
                down_copy(d).start()

        in_up = (u >= 0) & (u < units)
        in_down = (d >= 0) & (d < units)
        low = level < levels // 2
        pl.when(in_down & jnp.logical_not(low))(downward)
        pl.when(in_up)(upward)
        pl.when(in_down & low)(downward)
        w = t - far_off

        @pl.when((w >= 0) & (w < units))
        def _():
            own_ref[w % EPOCHS, 2 * (w // EPOCHS) + column] = jnp.where(
                choose(flag[2], w % EPOCHS), down_in[w], up_out[w]
            )
            post_copy(w).start()
            core_copy(w, False).start()

        x = t - far_off - POST

        @pl.when((x >= 0) & (x < units))
        def _():
            post_copy(x).wait_recv()
            core_copy(x, True).start()

        def settle(n, relayed):
            @pl.when((n >= 0) & (n < units))
            def _():
                core_copy(n, relayed).wait_recv()
                arrange(n % EPOCHS, 2 * (n // EPOCHS) + ((1 - column) if relayed else column))
                if not relayed:
                    return

                @pl.when(level < levels - 1)
                def _():
                    up_copy(n).wait_send()

                @pl.when(level > 0)
                def _():
                    down_copy(n).wait_send()

                post_copy(n).wait_send()
                core_copy(n, False).wait_send()
                core_copy(n, True).wait_send()

        settle(t - far_off - CORE, False)
        settle(t - far_off - POST - CORE, True)
        return carry

    def slots(first, last):
        lax.fori_loop(first, last, slot, 0)

    pieces = [
        functools.partial(weights, 1, 0, ksize // 2),
        functools.partial(weights, 1, ksize // 2, ksize),
        functools.partial(operands, 1, 0, depth // 2),
        functools.partial(operands, 1, depth // 2, depth),
    ]
    cuts = [products * i // 4 for i in range(5)]
    pieces += [functools.partial(correlate, 1, cuts[i], cuts[i + 1]) for i in range(4)]
    for t, piece in enumerate(pieces):
        slots(t, t + 1)
        piece()
    slots(len(pieces), units + LAG * (levels - 1) + POST + CORE)

    for k in range(halves):
        pre_copy(k).wait_send()


def search(image, variance, kernel, epoch_owner, valid_rows, blocks):
    ksize = kernel.shape[0]
    band = image.shape[0] // blocks
    per = band * blocks // LANES
    half = ksize // 2
    chunks = 2 * per
    units = chunks // 2 * EPOCHS
    tiles = (ksize + 1) // 2 + -(-(ksize + 1) // 8)
    vmem = pl.BlockSpec(memory_space=pltpu.VMEM)
    plane = (LANES, LANES)
    held = (2 * EPOCHS, per + 2 * MAXS, LANES + 2 * MAXS, LANES)
    dma = pltpu.SemaphoreType.DMA
    depth = 6 * LANES
    return pl.pallas_call(
        functools.partial(search_kernel, ksize),
        out_shape=pltpu.VMEM(held, jnp.float32),
        in_specs=[pl.BlockSpec(memory_space=pltpu.HBM)] * 5,
        out_specs=vmem,
        scratch_shapes=[
            pltpu.SMEM(epoch_owner.shape, jnp.int32),
            pltpu.SMEM(valid_rows.shape[::-1], jnp.int32),
            pltpu.VMEM(kernel.shape, jnp.float32),
            pltpu.VMEM(image.shape, jnp.float32),
            pltpu.VMEM(image.shape, jnp.float32),
            dma((5,)),
            pltpu.VMEM((ksize + -ksize % 8, LANES), jnp.float32),
            pltpu.VMEM((EPOCHS, chunks) + plane, jnp.float32),
            pltpu.VMEM((EPOCHS, chunks) + plane, jnp.float32),
            pltpu.VMEM((2, band + 2 * half + 2, blocks, LANES), jnp.float32),
            pltpu.VMEM((2, band // 2 + half, blocks, depth), jnp.bfloat16),
            pltpu.VMEM((2, band // 2 + half + 2, blocks, depth), jnp.bfloat16),
            pltpu.VMEM((2, tiles, depth, 2 * LANES), jnp.bfloat16),
            pltpu.VMEM((band // 2 * blocks, 2 * LANES), jnp.float32),
            pltpu.VMEM((chunks,) + plane, jnp.float32),
            pltpu.VMEM((chunks // 2,) + plane, jnp.float32),
        ]
        + [pltpu.VMEM((units,) + plane, jnp.float32)] * 4
        + [dma((2,))] * 2
        + [dma((chunks // 2,))] * 2
        + [dma((units,))] * 6
        + [dma((EPOCHS, chunks))] * 2,
        compiler_params=pltpu.CompilerParams(
            collective_id=0, has_side_effects=True, vmem_limit_bytes=34 * 2**20
        ),
        name="search",
    )(*[
        pltpu.with_memory_space_constraint(x, pltpu.HBM)
        for x in (epoch_owner, valid_rows.T, kernel, image, variance)
    ])


def stack_kernel(shift_ref, kernel_ref, held, out_ref, made, sem):
    velocities = out_ref.shape[0]
    per = held.shape[1] - 2 * MAXS
    slots = made.shape[0]
    kernel = kernel_ref[...]
    norm = kernel / jnp.sum(kernel)
    floor = 0.5 * jnp.sum(norm * norm)

    def copy(v):
        return pltpu.make_async_copy(made.at[v % slots], out_ref.at[v], sem.at[v % slots])

    def one(v, carry):
        @pl.when(v >= slots)
        def _():
            copy(v - slots).wait()

        places = [(MAXS + shift_ref[e, 0, v], MAXS + shift_ref[e, 1, v]) for e in range(EPOCHS)]
        target = made.at[v % slots]
        for i in range(per):
            sums = []
            for f in range(2):
                total = None
                for e in range(EPOCHS):
                    value = held[2 * e + f, places[e][0] + i, pl.ds(places[e][1], LANES), :]
                    total = value if total is None else total + value
                sums.append(total)
            value = sums[0] * lax.rsqrt(jnp.maximum(sums[1], floor))
            target[pl.ds(i, LANES, stride=per), :] = value.T
        copy(v).start()
        return carry

    lax.fori_loop(0, velocities, one, 0)
    for v in range(velocities - slots, velocities):
        copy(v).wait()


def stack(held, shifts, kernel):
    velocities = shifts.shape[0]
    per = held.shape[1] - 2 * MAXS
    smem = pl.BlockSpec(memory_space=pltpu.SMEM)
    vmem = pl.BlockSpec(memory_space=pltpu.VMEM)
    slots = min(3, velocities)
    return pl.pallas_call(
        stack_kernel,
        out_shape=jax.ShapeDtypeStruct((velocities, LANES * per, LANES), jnp.float32),
        in_specs=[smem, vmem, vmem],
        out_specs=pl.BlockSpec(memory_space=pl.ANY),
        scratch_shapes=[
            pltpu.VMEM((slots, LANES * per, LANES), jnp.float32),
            pltpu.SemaphoreType.DMA((slots,)),
        ],
        compiler_params=pltpu.CompilerParams(vmem_limit_bytes=8 * 2**20),
        name="stack",
    )(shifts.transpose(1, 2, 0), kernel, held)


def local(images, variance, spread_kernel, shifts, epoch_owner, valid_rows):
    band, columns = images.shape[1:]
    blocks = columns // LANES
    groups = LANES // blocks
    per = band // groups

    def tiled(array):
        return array.reshape(groups, per, blocks, LANES).transpose(0, 2, 1, 3).reshape(-1, LANES)

    held = search(tiled(images), tiled(variance), spread_kernel, epoch_owner, valid_rows, blocks)
    out = stack(held, shifts, spread_kernel)
    out = out.reshape(-1, groups, blocks, per, LANES).transpose(0, 1, 3, 2, 4)
    return out.reshape(-1, band, columns)


def solution(mesh):
    in_specs = (
        P(("fields", "vel"), "rows", None),
        P(("fields", "vel"), "rows", None),
        P(),
        P(("fields", "vel"), None, None),
        P("fields"),
        P("fields", None),
    )
    out_specs = P(("fields", "vel"), "rows", None)
    return jax.shard_map(local, mesh=mesh, in_specs=in_specs, out_specs=out_specs, check_vma=False)
```

```python
import functools

import jax
import jax.numpy as jnp
from jax import lax
from jax.experimental import pallas as pl
from jax.experimental.pallas import tpu as pltpu
from jax.sharding import PartitionSpec as P

MAXS = 16
EPOCHS = 3
LANES = 128
SIDE = 16
LAG = 3
POST = 8
CORE = 2
GROUP = 6
MESH = pl.DeviceIdType.MESH


def split(value):
    high = value.astype(jnp.bfloat16)
    return high, (value - high.astype(jnp.float32)).astype(jnp.bfloat16)


def lanes_of(shape):
    return lax.broadcasted_iota(jnp.int32, shape, len(shape) - 1)


def search_kernel(
    ksize, owner_in, valid_in, kernel_in, image_in, variance_in,
    held_ref,
    owner_ref, valid_ref, kernel_ref, image_ref, variance_ref, load_sem,
    taps_ref, own_ref, other_ref, rows_buf, left, sides, weight, acc, mine, near, up_in, up_out, down_in, down_out,
    halo_send, halo_recv, pre_send, pre_recv, up_send, up_recv, down_send, down_recv,
    post_send, post_recv, core_send, core_recv,
):
    count = lax.axis_size("vel")
    levels = count // 2
    me, core = lax.axis_index("vel"), lax.axis_index("rows")
    level, column = me // 2, me % 2
    peer = {"vel": 2 * level + 1 - column}
    above = {"vel": jnp.minimum(me + 2, count - 1)}
    below = {"vel": jnp.maximum(me - 2, 0)}
    twin = {"rows": 1 - core}
    half = ksize // 2
    blocks = rows_buf.shape[2]
    groups = LANES // blocks
    band = image_ref.shape[0] // blocks
    per = band // groups
    pairs = band // 2
    chunks = 2 * per
    halves = chunks // 2
    units = halves * EPOCHS

    loads = [
        pltpu.make_async_copy(source, target, load_sem.at[i])
        for i, (source, target) in enumerate(
            (
                (owner_in, owner_ref),
                (valid_in, valid_ref),
                (image_in, image_ref),
                (variance_in, variance_ref),
                (kernel_in, kernel_ref),
            )
        )
    ]
    for load in loads:
        load.start()

    barrier = pltpu.get_barrier_semaphore()

    def greet(target):
        pl.semaphore_signal(barrier, inc=1, device_id=target, device_id_type=MESH)

    greet(peer)
    greet(twin)

    @pl.when(level > 0)
    def _():
        greet(below)

    @pl.when(level < levels - 1)
    def _():
        greet(above)

    for load in loads:
        load.wait()

    lower = jnp.int32(0)
    upper = jnp.int32(0)
    holds, close, over = [], [], []
    for e in range(EPOCHS):
        owner = owner_ref[e]
        lower += jnp.where(owner == me, valid_ref[0, e], 0)
        upper += jnp.where(owner == me, valid_ref[1, e], 0)
        holds.append(owner == me)
        close.append(owner // 2 == level)
        over.append(owner // 2 > level)

    def fill(y, carry):
        place = pl.ds((y // per) * (blocks * per) + y % per, blocks, stride=per)
        row = core * band + y
        usable = (row >= lower) & (row < upper)
        noise = 1.0 / variance_ref[place, :]
        rows_buf[0, half + y] = jnp.where(usable, image_ref[place, :] * noise, 0.0)
        rows_buf[1, half + y] = jnp.where(usable, noise, 0.0)
        return carry

    edge = (1 - core) * (band - half)
    lax.fori_loop(0, half, lambda y, carry: fill(edge + y, carry), 0, unroll=5)

    @pl.when((level > 0) & (level < levels - 1))
    def _():
        pl.semaphore_wait(barrier, 4)

    @pl.when((level == 0) | (level == levels - 1))
    def _():
        pl.semaphore_wait(barrier, 3)

    halo = []
    for f in range(2):
        copy = pltpu.make_async_remote_copy(
            src_ref=rows_buf.at[f, pl.ds(half + edge, half)],
            dst_ref=rows_buf.at[f, pl.ds(core * (half + band), half)],
            send_sem=halo_send.at[f],
            recv_sem=halo_recv.at[f],
            device_id=twin,
            device_id_type=MESH,
        )
        copy.start()
        halo.append(copy)
    lax.fori_loop(0, band - half, lambda y, carry: fill(core * half + y, carry), 0, unroll=11)
    empty = jnp.zeros((half, blocks, LANES), jnp.float32)
    for f in range(2):
        rows_buf[f, pl.ds(core * (half + band), half)] = empty
        rows_buf[f, 2 * half + band :] = jnp.zeros((2, blocks, LANES), jnp.float32)

    taps_ref[...] = jnp.zeros_like(taps_ref)
    kernel = kernel_ref[...]
    taps_ref[:ksize, :ksize] = kernel / jnp.sum(kernel)
    spot = lanes_of((8, LANES))
    spot = jnp.where(spot <= half, half - spot, jnp.where(spot >= LANES - half, half + LANES - spot, LANES - 1))
    norm = jnp.concatenate(
        [
            jnp.take_along_axis(taps_ref[8 * g : 8 * g + 8, :], spot, axis=1)
            for g in range(taps_ref.shape[0] // 8)
        ],
        axis=0,
    )
    row_at = lax.broadcasted_iota(jnp.int32, (LANES, LANES), 0)
    lane_at = lanes_of((LANES, LANES))
    inside = jnp.abs(row_at - lane_at) < LANES // 2
    left_in = lanes_of((SIDE, LANES)) < LANES // 2
    tiles = (ksize + 1) // 2
    window = 2 * LANES

    def put(f, tile, row, half_at, value):
        size = value.shape[0]
        high, low = split(value)
        columns = slice(half_at * LANES, (half_at + 1) * LANES)
        weight[f, tile, row : row + size, columns] = high
        weight[f, tile, window + row : window + row + size, columns] = high
        weight[f, tile, 2 * window + row : 2 * window + row + size, columns] = low

    def weights(f, first, last):
        values = norm if f == 0 else norm * norm
        for a in range(ksize + 1 + (-(ksize + 1)) % 8):
            for p in range(2):
                if first == 0 and (a - p < 0 or a - p >= ksize):
                    if a <= ksize:
                        put(f, a // 2, (a % 2) * LANES, p, jnp.zeros((LANES, LANES), jnp.float32))
                    put(f, tiles + a // 8, (a % 8) * 2 * SIDE, p, jnp.zeros((2 * SIDE, LANES), jnp.float32))
        for a in range(first, last):
            base = jnp.broadcast_to(values[a : a + 1, :], (8, LANES))
            base = pltpu.roll(base, 0, 1, stride=1, stride_axis=0)
            ring = jnp.concatenate([base if g == 0 else pltpu.roll(base, 8 * g, 1) for g in range(LANES // 8)], axis=0)
            own = jnp.where(inside, ring, 0.0)
            side = jnp.concatenate(
                [
                    jnp.where(left_in, ring[LANES - SIDE :], 0.0),
                    jnp.where(left_in, 0.0, ring[:SIDE]),
                ],
                axis=0,
            )
            for p in range(2):
                at = a + p
                put(f, at // 2, (at % 2) * LANES, p, own)
                put(f, tiles + at // 8, (at % 8) * 2 * SIDE, p, side)

    weights(0, 0, ksize)

    lane = lanes_of((blocks, LANES))
    block_at = lax.broadcasted_iota(jnp.int32, (blocks, LANES), 0)

    def beside(value):
        before = jnp.where(block_at == 0, 0.0, pltpu.roll(value, 1, 0))
        after = jnp.where(block_at == blocks - 1, 0.0, pltpu.roll(value, blocks - 1, 0))
        return jnp.where(lane >= LANES - SIDE, before, jnp.where(lane < SIDE, after, 0.0))

    def gathered(f, m):
        first = pltpu.roll(beside(rows_buf[f, 2 * m]), SIDE, 1)
        second = pltpu.roll(beside(rows_buf[f, 2 * m + 1]), 3 * SIDE, 1)
        return first + second

    def store(ref, f, m, at, value):
        high, low = split(value)
        columns = slice(at * LANES, (at + 1) * LANES)
        ref[f, m, :, columns] = high
        ref[f, m, :, window + at * LANES : window + (at + 1) * LANES] = low
        ref[f, m, :, 2 * window + at * LANES : 2 * window + (at + 1) * LANES] = high

    def operands(f, first, last, base=0):
        def step(m, this):
            for p in range(2):
                store(left, f, m, p, rows_buf[f, 2 * m + p])
            following = gathered(f, m + 1)
            both = this + pltpu.roll(following, LANES // 2, 1)
            store(sides, f, m + 2, 0, both)
            store(sides, f, m, 1, both)
            return following

        start = gathered(f, base + first)
        lax.fori_loop(first, last, lambda m, carry: step(base + m, carry), start, unroll=last - first)

    products = weight.shape[1]

    def product(f, ref, m, j):
        value = ref[f, pl.ds(m, pairs)].reshape(pairs * blocks, 3 * window)
        return jnp.dot(value, weight[f, j], preferred_element_type=jnp.float32)

    def correlate(f, first, last):
        for j in range(first, last):
            value = product(f, left, j, j) if j < tiles else product(f, sides, 2 + 4 * (j - tiles), j)
            if j == 0:
                acc[...] = value
            else:
                acc[...] += value
        if last < products:
            return
        for i in range(per):
            q, p = i // 2, i % 2
            part = [
                acc[(r * (per // 2) + q) * blocks : (r * (per // 2) + q + 1) * blocks, p * LANES : (p + 1) * LANES]
                for r in range(groups)
            ]
            mine[f * per + i] = jnp.concatenate(part, axis=0).T
        for k in range(f * per // 2, (f + 1) * per // 2):
            pre_copy(k).start()

    def pre_copy(k):
        return pltpu.make_async_remote_copy(
            src_ref=mine.at[2 * k + 1 - column],
            dst_ref=near.at[k],
            send_sem=pre_send.at[k],
            recv_sem=pre_recv.at[k],
            device_id=peer,
            device_id_type=MESH,
        )

    depth = half + pairs
    alone = depth - half // 2 - 1
    operands(0, 0, alone, core * (depth - alone))
    ready = alone - pairs + 1
    first = core * (tiles - ready)
    acc[...] = product(0, left, first, first)
    for i in range(1, ready):
        acc[...] += product(0, left, first + i, first + i)
    for copy in halo:
        copy.wait()
    operands(0, 0, depth - alone, (1 - core) * alone)
    first = (1 - core) * ready
    for i in range(tiles - ready):
        acc[...] += product(0, left, first + i, first + i)
    correlate(0, tiles, products)

    def hop(source, target, send, recv, to):
        def make(u):
            return pltpu.make_async_remote_copy(
                src_ref=source.at[u],
                dst_ref=target.at[u],
                send_sem=send.at[u],
                recv_sem=recv.at[u],
                device_id=to,
                device_id_type=MESH,
            )

        return make

    up_copy = hop(up_out, up_in, up_send, up_recv, above)
    down_copy = hop(down_out, down_in, down_send, down_recv, below)

    def post_copy(u):
        e, c = u % EPOCHS, 2 * (u // EPOCHS) + column
        return pltpu.make_async_remote_copy(
            src_ref=own_ref.at[e, c],
            dst_ref=own_ref.at[e, c],
            send_sem=post_send.at[u],
            recv_sem=post_recv.at[u],
            device_id=peer,
            device_id_type=MESH,
        )

    def core_copy(u, relayed):
        e = u % EPOCHS
        c = 2 * (u // EPOCHS) + ((1 - column) if relayed else column)
        return pltpu.make_async_remote_copy(
            src_ref=own_ref.at[e, c],
            dst_ref=other_ref.at[e, c],
            send_sem=core_send.at[e, c],
            recv_sem=core_recv.at[e, c],
            device_id=twin,
            device_id_type=MESH,
        )

    def choose(flags, e):
        value = flags[EPOCHS - 1]
        for i in range(EPOCHS - 1):
            value = jnp.where(e == i, flags[i], value)
        return value != 0

    flag = [[jnp.where(x, 1, 0) for x in flags] for flags in (holds, close, over)]
    up_off = LAG * level
    down_off = LAG * (levels - 1 - level)
    near_off = jnp.minimum(up_off, down_off)
    far_off = jnp.maximum(up_off, down_off)

    def known(u, arrived):
        k, e = u // EPOCHS, u % EPOCHS
        local_value = jnp.where(choose(flag[0], e), mine[2 * k + column], near[k])
        return jnp.where(choose(flag[1], e), local_value, arrived)

    side_block = lanes_of((MAXS, LANES)) % blocks
    at_first = core == 0

    def arrange(e, c):
        here = own_ref[e, c]
        there = other_ref[e, c]
        before = jnp.where(at_first, 0.0, there)
        after = jnp.where(at_first, there, 0.0)
        span = MAXS // per
        for p in range(2 * span + 1):
            move = (span - p) * blocks
            if move > 0:
                value = pltpu.roll(jnp.where(lane_at < LANES - move, here, before), move, 1)
            elif move < 0:
                value = pltpu.roll(jnp.where(lane_at < -move, after, here), LANES + move, 1)
            else:
                value = here
            target = held_ref.at[2 * e + c // per, p * per + c % per]
            target[MAXS : MAXS + LANES] = value
            target[:MAXS] = jnp.where(side_block == 0, 0.0, pltpu.roll(value[LANES - MAXS :], 1, 1))
            target[MAXS + LANES :] = jnp.where(
                side_block == blocks - 1, 0.0, pltpu.roll(value[:MAXS], LANES - 1, 1)
            )

    def slot(t, carry):
        first = t - near_off

        @pl.when((first >= 0) & (first < units) & (first % EPOCHS == 0))
        def _():
            pre_copy(first // EPOCHS).wait_recv()

        u = t - up_off

        def upward():
            @pl.when(level > 0)
            def _():
                up_copy(u).wait_recv()

            up_out[u] = known(u, up_in[u])

            @pl.when(level < levels - 1)
            def _():
                up_copy(u).start()

        d = t - down_off

        def downward():
            @pl.when(level < levels - 1)
            def _():
                down_copy(d).wait_recv()

            @pl.when(level > 0)
            def _():
                down_out[d] = known(d, down_in[d])
                down_copy(d).start()

        in_up = (u >= 0) & (u < units)
        in_down = (d >= 0) & (d < units)
        low = level < levels // 2
        pl.when(in_down & jnp.logical_not(low))(downward)
        pl.when(in_up)(upward)
        pl.when(in_down & low)(downward)
        w = t - far_off

        @pl.when((w >= 0) & (w < units))
        def _():
            own_ref[w % EPOCHS, 2 * (w // EPOCHS) + column] = jnp.where(
                choose(flag[2], w % EPOCHS), down_in[w], up_out[w]
            )
            post_copy(w).start()
            core_copy(w, False).start()

        x = t - far_off - POST

        @pl.when((x >= 0) & (x < units))
        def _():
            post_copy(x).wait_recv()
            core_copy(x, True).start()

        def settle(n, relayed):
            @pl.when((n >= 0) & (n < units))
            def _():
                core_copy(n, relayed).wait_recv()
                arrange(n % EPOCHS, 2 * (n // EPOCHS) + ((1 - column) if relayed else column))
                if not relayed:
                    return

                @pl.when(level < levels - 1)
                def _():
                    up_copy(n).wait_send()

                @pl.when(level > 0)
                def _():
                    down_copy(n).wait_send()

                post_copy(n).wait_send()
                core_copy(n, False).wait_send()
                core_copy(n, True).wait_send()

        settle(t - far_off - CORE, False)
        settle(t - far_off - POST - CORE, True)
        return carry

    def slots(first, last):
        lax.fori_loop(first, last, slot, 0)

    pieces = [
        functools.partial(weights, 1, 0, ksize // 2),
        functools.partial(weights, 1, ksize // 2, ksize),
        functools.partial(operands, 1, 0, depth // 2),
        functools.partial(operands, 1, depth // 2, depth),
    ]
    cuts = [products * i // 4 for i in range(5)]
    pieces += [functools.partial(correlate, 1, cuts[i], cuts[i + 1]) for i in range(4)]
    for t, piece in enumerate(pieces):
        slots(t, t + 1)
        piece()
    slots(len(pieces), units + LAG * (levels - 1) + POST + CORE)

    for k in range(halves):
        pre_copy(k).wait_send()


def search(image, variance, kernel, epoch_owner, valid_rows, blocks):
    ksize = kernel.shape[0]
    band = image.shape[0] // blocks
    per = band * blocks // LANES
    half = ksize // 2
    chunks = 2 * per
    units = chunks // 2 * EPOCHS
    tiles = (ksize + 1) // 2 + -(-(ksize + 1) // 8)
    vmem = pl.BlockSpec(memory_space=pltpu.VMEM)
    plane = (LANES, LANES)
    held = (2 * EPOCHS, per + 2 * MAXS, LANES + 2 * MAXS, LANES)
    dma = pltpu.SemaphoreType.DMA
    depth = 6 * LANES
    return pl.pallas_call(
        functools.partial(search_kernel, ksize),
        out_shape=pltpu.VMEM(held, jnp.float32),
        in_specs=[pl.BlockSpec(memory_space=pltpu.HBM)] * 5,
        out_specs=vmem,
        scratch_shapes=[
            pltpu.SMEM(epoch_owner.shape, jnp.int32),
            pltpu.SMEM(valid_rows.shape[::-1], jnp.int32),
            pltpu.VMEM(kernel.shape, jnp.float32),
            pltpu.VMEM(image.shape, jnp.float32),
            pltpu.VMEM(image.shape, jnp.float32),
            dma((5,)),
            pltpu.VMEM((ksize + -ksize % 8, LANES), jnp.float32),
            pltpu.VMEM((EPOCHS, chunks) + plane, jnp.float32),
            pltpu.VMEM((EPOCHS, chunks) + plane, jnp.float32),
            pltpu.VMEM((2, band + 2 * half + 2, blocks, LANES), jnp.float32),
            pltpu.VMEM((2, band // 2 + half, blocks, depth), jnp.bfloat16),
            pltpu.VMEM((2, band // 2 + half + 2, blocks, depth), jnp.bfloat16),
            pltpu.VMEM((2, tiles, depth, 2 * LANES), jnp.bfloat16),
            pltpu.VMEM((band // 2 * blocks, 2 * LANES), jnp.float32),
            pltpu.VMEM((chunks,) + plane, jnp.float32),
            pltpu.VMEM((chunks // 2,) + plane, jnp.float32),
        ]
        + [pltpu.VMEM((units,) + plane, jnp.float32)] * 4
        + [dma((2,))] * 2
        + [dma((chunks // 2,))] * 2
        + [dma((units,))] * 6
        + [dma((EPOCHS, chunks))] * 2,
        compiler_params=pltpu.CompilerParams(
            collective_id=0, has_side_effects=True, vmem_limit_bytes=34 * 2**20
        ),
        name="search",
    )(*[
        pltpu.with_memory_space_constraint(x, pltpu.HBM)
        for x in (epoch_owner, valid_rows.T, kernel, image, variance)
    ])


def stack_kernel(shift_ref, kernel_ref, held, out_ref, made, sem):
    velocities = out_ref.shape[0]
    per = held.shape[1] - 2 * MAXS
    slots = made.shape[0]
    kernel = kernel_ref[...]
    norm = kernel / jnp.sum(kernel)
    floor = 0.5 * jnp.sum(norm * norm)

    group = made.shape[1]
    steps = velocities // group

    def copy(t):
        return pltpu.make_async_copy(
            made.at[t % slots], out_ref.at[pl.ds(t * group, group)], sem.at[t % slots]
        )

    def one(target, v):
        places = [(MAXS + shift_ref[e, 0, v], MAXS + shift_ref[e, 1, v]) for e in range(EPOCHS)]
        for i in range(per):
            sums = []
            for f in range(2):
                total = None
                for e in range(EPOCHS):
                    value = held[2 * e + f, places[e][0] + i, pl.ds(places[e][1], LANES), :]
                    total = value if total is None else total + value
                sums.append(total)
            value = sums[0] * lax.rsqrt(jnp.maximum(sums[1], floor))
            target[pl.ds(i, LANES, stride=per), :] = value.T

    def step(t, carry):
        @pl.when(t >= slots)
        def _():
            copy(t - slots).wait()

        for g in range(group):
            one(made.at[t % slots, g], t * group + g)
        copy(t).start()
        return carry

    lax.fori_loop(0, steps, step, 0)
    for t in range(max(steps - slots, 0), steps):
        copy(t).wait()


def stack(held, shifts, kernel):
    velocities = shifts.shape[0]
    per = held.shape[1] - 2 * MAXS
    smem = pl.BlockSpec(memory_space=pltpu.SMEM)
    vmem = pl.BlockSpec(memory_space=pltpu.VMEM)
    group = max(g for g in range(1, GROUP + 1) if velocities % g == 0)
    slots = min(2, velocities // group)
    return pl.pallas_call(
        stack_kernel,
        out_shape=jax.ShapeDtypeStruct((velocities, LANES * per, LANES), jnp.float32),
        in_specs=[smem, vmem, vmem],
        out_specs=pl.BlockSpec(memory_space=pl.ANY),
        scratch_shapes=[
            pltpu.VMEM((slots, group, LANES * per, LANES), jnp.float32),
            pltpu.SemaphoreType.DMA((slots,)),
        ],
        compiler_params=pltpu.CompilerParams(vmem_limit_bytes=8 * 2**20),
        name="stack",
    )(shifts.transpose(1, 2, 0), kernel, held)


def local(images, variance, spread_kernel, shifts, epoch_owner, valid_rows):
    band, columns = images.shape[1:]
    blocks = columns // LANES
    groups = LANES // blocks
    per = band // groups

    def tiled(array):
        return array.reshape(groups, per, blocks, LANES).transpose(0, 2, 1, 3).reshape(-1, LANES)

    held = search(tiled(images), tiled(variance), spread_kernel, epoch_owner, valid_rows, blocks)
    out = stack(held, shifts, spread_kernel)
    out = out.reshape(-1, groups, blocks, per, LANES).transpose(0, 1, 3, 2, 4)
    return out.reshape(-1, band, columns)


def solution(mesh):
    in_specs = (
        P(("fields", "vel"), "rows", None),
        P(("fields", "vel"), "rows", None),
        P(),
        P(("fields", "vel"), None, None),
        P("fields"),
        P("fields", None),
    )
    out_specs = P(("fields", "vel"), "rows", None)
    return jax.shard_map(local, mesh=mesh, in_specs=in_specs, out_specs=out_specs, check_vma=False)
```

```python
import functools

import jax
import jax.numpy as jnp
from jax import lax
from jax.experimental import pallas as pl
from jax.experimental.pallas import tpu as pltpu
from jax.sharding import PartitionSpec as P

MAXS = 16
EPOCHS = 3
LANES = 128
SIDE = 16
LAG = 3
POST = 8
CORE = 2
GROUP = 6
MESH = pl.DeviceIdType.MESH


def split(value):
    high = value.astype(jnp.bfloat16)
    return high, (value - high.astype(jnp.float32)).astype(jnp.bfloat16)


def lanes_of(shape):
    return lax.broadcasted_iota(jnp.int32, shape, len(shape) - 1)


def search_kernel(
    ksize, owner_in, valid_in, kernel_in, image_in, variance_in,
    held_ref,
    owner_ref, valid_ref, kernel_ref, image_ref, variance_ref, load_sem,
    taps_ref, own_ref, other_ref, rows_buf, left, sides, weight, acc, mine, near, up_in, up_out, down_in, down_out,
    halo_send, halo_recv, pre_send, pre_recv, up_send, up_recv, down_send, down_recv,
    post_send, post_recv, core_send, core_recv,
):
    count = lax.axis_size("vel")
    levels = count // 2
    me, core = lax.axis_index("vel"), lax.axis_index("rows")
    level, column = me // 2, me % 2
    peer = {"vel": 2 * level + 1 - column}
    above = {"vel": jnp.minimum(me + 2, count - 1)}
    below = {"vel": jnp.maximum(me - 2, 0)}
    twin = {"rows": 1 - core}
    half = ksize // 2
    blocks = rows_buf.shape[2]
    groups = LANES // blocks
    band = image_ref.shape[0] // blocks
    per = band // groups
    pairs = band // 2
    chunks = 2 * per
    halves = chunks // 2
    units = halves * EPOCHS

    loads = [
        pltpu.make_async_copy(source, target, load_sem.at[i])
        for i, (source, target) in enumerate(
            (
                (owner_in, owner_ref),
                (valid_in, valid_ref),
                (image_in, image_ref),
                (variance_in, variance_ref),
                (kernel_in, kernel_ref),
            )
        )
    ]
    for load in loads:
        load.start()

    barrier = pltpu.get_barrier_semaphore()

    def greet(target):
        pl.semaphore_signal(barrier, inc=1, device_id=target, device_id_type=MESH)

    greet(peer)
    greet(twin)

    @pl.when(level > 0)
    def _():
        greet(below)

    @pl.when(level < levels - 1)
    def _():
        greet(above)

    for load in loads:
        load.wait()

    lower = jnp.int32(0)
    upper = jnp.int32(0)
    holds, close, over = [], [], []
    for e in range(EPOCHS):
        owner = owner_ref[e]
        lower += jnp.where(owner == me, valid_ref[0, e], 0)
        upper += jnp.where(owner == me, valid_ref[1, e], 0)
        holds.append(owner == me)
        close.append(owner // 2 == level)
        over.append(owner // 2 > level)

    def fill(y, carry):
        place = pl.ds((y // per) * (blocks * per) + y % per, blocks, stride=per)
        row = core * band + y
        usable = (row >= lower) & (row < upper)
        noise = 1.0 / variance_ref[place, :]
        rows_buf[0, half + y] = jnp.where(usable, image_ref[place, :] * noise, 0.0)
        rows_buf[1, half + y] = jnp.where(usable, noise, 0.0)
        return carry

    edge = (1 - core) * (band - half)
    lax.fori_loop(0, half, lambda y, carry: fill(edge + y, carry), 0, unroll=5)

    @pl.when((level > 0) & (level < levels - 1))
    def _():
        pl.semaphore_wait(barrier, 4)

    @pl.when((level == 0) | (level == levels - 1))
    def _():
        pl.semaphore_wait(barrier, 3)

    halo = []
    for f in range(2):
        copy = pltpu.make_async_remote_copy(
            src_ref=rows_buf.at[f, pl.ds(half + edge, half)],
            dst_ref=rows_buf.at[f, pl.ds(core * (half + band), half)],
            send_sem=halo_send.at[f],
            recv_sem=halo_recv.at[f],
            device_id=twin,
            device_id_type=MESH,
        )
        copy.start()
        halo.append(copy)
    lax.fori_loop(0, band - half, lambda y, carry: fill(core * half + y, carry), 0, unroll=11)
    empty = jnp.zeros((half, blocks, LANES), jnp.float32)
    for f in range(2):
        rows_buf[f, pl.ds(core * (half + band), half)] = empty
        rows_buf[f, 2 * half + band :] = jnp.zeros((2, blocks, LANES), jnp.float32)

    taps_ref[...] = jnp.zeros_like(taps_ref)
    kernel = kernel_ref[...]
    taps_ref[:ksize, :ksize] = kernel / jnp.sum(kernel)
    spot = lanes_of((8, LANES))
    spot = jnp.where(spot <= half, half - spot, jnp.where(spot >= LANES - half, half + LANES - spot, LANES - 1))
    norm = jnp.concatenate(
        [
            jnp.take_along_axis(taps_ref[8 * g : 8 * g + 8, :], spot, axis=1)
            for g in range(taps_ref.shape[0] // 8)
        ],
        axis=0,
    )
    row_at = lax.broadcasted_iota(jnp.int32, (LANES, LANES), 0)
    lane_at = lanes_of((LANES, LANES))
    inside = jnp.abs(row_at - lane_at) < LANES // 2
    left_in = lanes_of((SIDE, LANES)) < LANES // 2
    tiles = (ksize + 1) // 2
    window = 2 * LANES

    def put(f, tile, row, half_at, value):
        size = value.shape[0]
        high, low = split(value)
        columns = slice(half_at * LANES, (half_at + 1) * LANES)
        weight[f, tile, row : row + size, columns] = high
        weight[f, tile, window + row : window + row + size, columns] = high
        weight[f, tile, 2 * window + row : 2 * window + row + size, columns] = low

    def weights(f, first, last):
        values = norm if f == 0 else norm * norm
        for a in range(ksize + 1 + (-(ksize + 1)) % 8):
            for p in range(2):
                if first == 0 and (a - p < 0 or a - p >= ksize):
                    if a <= ksize:
                        put(f, a // 2, (a % 2) * LANES, p, jnp.zeros((LANES, LANES), jnp.float32))
                    put(f, tiles + a // 8, (a % 8) * 2 * SIDE, p, jnp.zeros((2 * SIDE, LANES), jnp.float32))
        for a in range(first, last):
            base = jnp.broadcast_to(values[a : a + 1, :], (8, LANES))
            base = pltpu.roll(base, 0, 1, stride=1, stride_axis=0)
            ring = jnp.concatenate([base if g == 0 else pltpu.roll(base, 8 * g, 1) for g in range(LANES // 8)], axis=0)
            own = jnp.where(inside, ring, 0.0)
            side = jnp.concatenate(
                [
                    jnp.where(left_in, ring[LANES - SIDE :], 0.0),
                    jnp.where(left_in, 0.0, ring[:SIDE]),
                ],
                axis=0,
            )
            for p in range(2):
                at = a + p
                put(f, at // 2, (at % 2) * LANES, p, own)
                put(f, tiles + at // 8, (at % 8) * 2 * SIDE, p, side)

    weights(0, 0, ksize)

    lane = lanes_of((blocks, LANES))
    block_at = lax.broadcasted_iota(jnp.int32, (blocks, LANES), 0)

    def beside(value):
        before = jnp.where(block_at == 0, 0.0, pltpu.roll(value, 1, 0))
        after = jnp.where(block_at == blocks - 1, 0.0, pltpu.roll(value, blocks - 1, 0))
        return jnp.where(lane >= LANES - SIDE, before, jnp.where(lane < SIDE, after, 0.0))

    def gathered(f, m):
        first = pltpu.roll(beside(rows_buf[f, 2 * m]), SIDE, 1)
        second = pltpu.roll(beside(rows_buf[f, 2 * m + 1]), 3 * SIDE, 1)
        return first + second

    def store(ref, f, m, at, value):
        high, low = split(value)
        columns = slice(at * LANES, (at + 1) * LANES)
        ref[f, m, :, columns] = high
        ref[f, m, :, window + at * LANES : window + (at + 1) * LANES] = low
        ref[f, m, :, 2 * window + at * LANES : 2 * window + (at + 1) * LANES] = high

    def operands(f, first, last, base=0):
        def step(m, this):
            for p in range(2):
                store(left, f, m, p, rows_buf[f, 2 * m + p])
            following = gathered(f, m + 1)
            both = this + pltpu.roll(following, LANES // 2, 1)
            store(sides, f, m + 2, 0, both)
            store(sides, f, m, 1, both)
            return following

        start = gathered(f, base + first)
        lax.fori_loop(first, last, lambda m, carry: step(base + m, carry), start, unroll=last - first)

    products = weight.shape[1]

    def product(f, ref, m, j):
        value = ref[f, pl.ds(m, pairs)].reshape(pairs * blocks, 3 * window)
        return jnp.dot(value, weight[f, j], preferred_element_type=jnp.float32)

    def correlate(f, first, last):
        for j in range(first, last):
            value = product(f, left, j, j) if j < tiles else product(f, sides, 2 + 4 * (j - tiles), j)
            if j == 0:
                acc[...] = value
            else:
                acc[...] += value
        if last < products:
            return
        for i in range(per):
            q, p = i // 2, i % 2
            part = [
                acc[(r * (per // 2) + q) * blocks : (r * (per // 2) + q + 1) * blocks, p * LANES : (p + 1) * LANES]
                for r in range(groups)
            ]
            mine[f * per + i] = jnp.concatenate(part, axis=0).T
        for k in range(f * per // 2, (f + 1) * per // 2):
            pre_copy(k).start()

    def pre_copy(k):
        return pltpu.make_async_remote_copy(
            src_ref=mine.at[2 * k + 1 - column],
            dst_ref=near.at[k],
            send_sem=pre_send.at[k],
            recv_sem=pre_recv.at[k],
            device_id=peer,
            device_id_type=MESH,
        )

    depth = half + pairs
    alone = depth - half // 2 - 1
    operands(0, 0, alone, core * (depth - alone))
    ready = alone - pairs + 1
    first = core * (tiles - ready)
    acc[...] = product(0, left, first, first)
    for i in range(1, ready):
        acc[...] += product(0, left, first + i, first + i)
    for copy in halo:
        copy.wait()
    operands(0, 0, depth - alone, (1 - core) * alone)
    first = (1 - core) * ready
    for i in range(tiles - ready):
        acc[...] += product(0, left, first + i, first + i)
    correlate(0, tiles, products)

    def hop(source, target, send, recv, to):
        def make(u):
            return pltpu.make_async_remote_copy(
                src_ref=source.at[u],
                dst_ref=target.at[u],
                send_sem=send.at[u],
                recv_sem=recv.at[u],
                device_id=to,
                device_id_type=MESH,
            )

        return make

    up_copy = hop(up_out, up_in, up_send, up_recv, above)
    down_copy = hop(down_out, down_in, down_send, down_recv, below)

    def post_copy(u):
        e, c = u % EPOCHS, 2 * (u // EPOCHS) + column
        return pltpu.make_async_remote_copy(
            src_ref=own_ref.at[e, c],
            dst_ref=own_ref.at[e, c],
            send_sem=post_send.at[u],
            recv_sem=post_recv.at[u],
            device_id=peer,
            device_id_type=MESH,
        )

    def core_copy(u, relayed):
        e = u % EPOCHS
        c = 2 * (u // EPOCHS) + ((1 - column) if relayed else column)
        return pltpu.make_async_remote_copy(
            src_ref=own_ref.at[e, c],
            dst_ref=other_ref.at[e, c],
            send_sem=core_send.at[e, c],
            recv_sem=core_recv.at[e, c],
            device_id=twin,
            device_id_type=MESH,
        )

    def choose(flags, e):
        value = flags[EPOCHS - 1]
        for i in range(EPOCHS - 1):
            value = jnp.where(e == i, flags[i], value)
        return value != 0

    flag = [[jnp.where(x, 1, 0) for x in flags] for flags in (holds, close, over)]
    up_off = LAG * level
    down_off = LAG * (levels - 1 - level)
    near_off = jnp.minimum(up_off, down_off)
    far_off = jnp.maximum(up_off, down_off)

    def known(u, arrived):
        k, e = u // EPOCHS, u % EPOCHS
        local_value = jnp.where(choose(flag[0], e), mine[2 * k + column], near[k])
        return jnp.where(choose(flag[1], e), local_value, arrived)

    side_block = lanes_of((MAXS, LANES)) % blocks
    at_first = core == 0

    def arrange(e, c):
        here = own_ref[e, c]
        there = other_ref[e, c]
        before = jnp.where(at_first, 0.0, there)
        after = jnp.where(at_first, there, 0.0)
        span = MAXS // per
        for p in range(2 * span + 1):
            move = (span - p) * blocks
            if move > 0:
                value = pltpu.roll(jnp.where(lane_at < LANES - move, here, before), move, 1)
            elif move < 0:
                value = pltpu.roll(jnp.where(lane_at < -move, after, here), LANES + move, 1)
            else:
                value = here
            target = held_ref.at[2 * e + c // per, p * per + c % per]
            target[MAXS : MAXS + LANES] = value
            target[:MAXS] = jnp.where(side_block == 0, 0.0, pltpu.roll(value[LANES - MAXS :], 1, 1))
            target[MAXS + LANES :] = jnp.where(
                side_block == blocks - 1, 0.0, pltpu.roll(value[:MAXS], LANES - 1, 1)
            )

    def slot(t, carry):
        first = t - near_off

        @pl.when((first >= 0) & (first < units) & (first % EPOCHS == 0))
        def _():
            pre_copy(first // EPOCHS).wait_recv()

        u = t - up_off

        def upward():
            @pl.when(level > 0)
            def _():
                up_copy(u).wait_recv()

            up_out[u] = known(u, up_in[u])

            @pl.when(level < levels - 1)
            def _():
                up_copy(u).start()

        d = t - down_off

        def downward():
            @pl.when(level < levels - 1)
            def _():
                down_copy(d).wait_recv()

            @pl.when(level > 0)
            def _():
                down_out[d] = known(d, down_in[d])
                down_copy(d).start()

        in_up = (u >= 0) & (u < units)
        in_down = (d >= 0) & (d < units)
        low = level < levels // 2
        pl.when(in_down & jnp.logical_not(low))(downward)
        pl.when(in_up)(upward)
        pl.when(in_down & low)(downward)
        w = t - far_off

        @pl.when((w >= 0) & (w < units))
        def _():
            own_ref[w % EPOCHS, 2 * (w // EPOCHS) + column] = jnp.where(
                choose(flag[2], w % EPOCHS), down_in[w], up_out[w]
            )
            post_copy(w).start()
            core_copy(w, False).start()

        x = t - far_off - POST

        @pl.when((x >= 0) & (x < units))
        def _():
            post_copy(x).wait_recv()
            core_copy(x, True).start()

        def settle(n, relayed):
            @pl.when((n >= 0) & (n < units))
            def _():
                core_copy(n, relayed).wait_recv()
                arrange(n % EPOCHS, 2 * (n // EPOCHS) + ((1 - column) if relayed else column))
                if not relayed:
                    return

                @pl.when(level < levels - 1)
                def _():
                    up_copy(n).wait_send()

                @pl.when(level > 0)
                def _():
                    down_copy(n).wait_send()

                post_copy(n).wait_send()
                core_copy(n, False).wait_send()
                core_copy(n, True).wait_send()

        settle(t - far_off - CORE, False)
        settle(t - far_off - POST - CORE, True)
        return carry

    def slots(first, last):
        lax.fori_loop(first, last, slot, 0)

    pieces = [
        functools.partial(weights, 1, 0, ksize // 2),
        functools.partial(weights, 1, ksize // 2, ksize),
        functools.partial(operands, 1, 0, depth // 2),
        functools.partial(operands, 1, depth // 2, depth),
    ]
    cuts = [products * i // 4 for i in range(5)]
    pieces += [functools.partial(correlate, 1, cuts[i], cuts[i + 1]) for i in range(4)]
    for t, piece in enumerate(pieces):
        slots(t, t + 1)
        piece()
    slots(len(pieces), units + LAG * (levels - 1) + POST + CORE)

    for k in range(halves):
        pre_copy(k).wait_send()


def search(image, variance, kernel, epoch_owner, valid_rows, blocks):
    ksize = kernel.shape[0]
    band = image.shape[0] // blocks
    per = band * blocks // LANES
    half = ksize // 2
    chunks = 2 * per
    units = chunks // 2 * EPOCHS
    tiles = (ksize + 1) // 2 + -(-(ksize + 1) // 8)
    vmem = pl.BlockSpec(memory_space=pltpu.VMEM)
    plane = (LANES, LANES)
    held = (2 * EPOCHS, per + 2 * MAXS, LANES + 2 * MAXS, LANES)
    dma = pltpu.SemaphoreType.DMA
    depth = 6 * LANES
    return pl.pallas_call(
        functools.partial(search_kernel, ksize),
        out_shape=pltpu.VMEM(held, jnp.float32),
        in_specs=[pl.BlockSpec(memory_space=pltpu.HBM)] * 5,
        out_specs=vmem,
        scratch_shapes=[
            pltpu.SMEM(epoch_owner.shape, jnp.int32),
            pltpu.SMEM(valid_rows.shape[::-1], jnp.int32),
            pltpu.VMEM(kernel.shape, jnp.float32),
            pltpu.VMEM(image.shape, jnp.float32),
            pltpu.VMEM(image.shape, jnp.float32),
            dma((5,)),
            pltpu.VMEM((ksize + -ksize % 8, LANES), jnp.float32),
            pltpu.VMEM((EPOCHS, chunks) + plane, jnp.float32),
            pltpu.VMEM((EPOCHS, chunks) + plane, jnp.float32),
            pltpu.VMEM((2, band + 2 * half + 2, blocks, LANES), jnp.float32),
            pltpu.VMEM((2, band // 2 + half, blocks, depth), jnp.bfloat16),
            pltpu.VMEM((2, band // 2 + half + 2, blocks, depth), jnp.bfloat16),
            pltpu.VMEM((2, tiles, depth, 2 * LANES), jnp.bfloat16),
            pltpu.VMEM((band // 2 * blocks, 2 * LANES), jnp.float32),
            pltpu.VMEM((chunks,) + plane, jnp.float32),
            pltpu.VMEM((chunks // 2,) + plane, jnp.float32),
        ]
        + [pltpu.VMEM((units,) + plane, jnp.float32)] * 4
        + [dma((2,))] * 2
        + [dma((chunks // 2,))] * 2
        + [dma((units,))] * 6
        + [dma((EPOCHS, chunks))] * 2,
        compiler_params=pltpu.CompilerParams(
            collective_id=0, has_side_effects=True, vmem_limit_bytes=34 * 2**20
        ),
        name="search",
    )(*[
        pltpu.with_memory_space_constraint(x, pltpu.HBM)
        for x in (epoch_owner, valid_rows.T, kernel, image, variance)
    ])


def stack_kernel(shift_ref, kernel_ref, held, out_ref, made, sem):
    velocities = out_ref.shape[0]
    per = held.shape[1] - 2 * MAXS
    slots = made.shape[0]
    kernel = kernel_ref[...]
    norm = kernel / jnp.sum(kernel)
    floor = 0.5 * jnp.sum(norm * norm)

    group = made.shape[1]
    steps = velocities // group

    def copy(t, g):
        return pltpu.make_async_copy(
            made.at[t % slots, g], out_ref.at[t * group + g], sem.at[t % slots, g]
        )

    def one(target, v):
        places = [(MAXS + shift_ref[e, 0, v], MAXS + shift_ref[e, 1, v]) for e in range(EPOCHS)]
        for i in range(per):
            sums = []
            for f in range(2):
                total = None
                for e in range(EPOCHS):
                    value = held[2 * e + f, places[e][0] + i, pl.ds(places[e][1], LANES), :]
                    total = value if total is None else total + value
                sums.append(total)
            value = sums[0] * lax.rsqrt(jnp.maximum(sums[1], floor))
            target[pl.ds(i, LANES, stride=per), :] = value.T

    def step(t, carry):
        @pl.when(t >= slots)
        def _():
            for g in range(group):
                copy(t - slots, g).wait()

        for g in range(group):
            one(made.at[t % slots, g], t * group + g)
            copy(t, g).start()
        return carry

    lax.fori_loop(0, steps, step, 0)
    for t in range(max(steps - slots, 0), steps):
        for g in range(group):
            copy(t, g).wait()


def stack(held, shifts, kernel):
    velocities = shifts.shape[0]
    per = held.shape[1] - 2 * MAXS
    smem = pl.BlockSpec(memory_space=pltpu.SMEM)
    vmem = pl.BlockSpec(memory_space=pltpu.VMEM)
    group = max(g for g in range(1, GROUP + 1) if velocities % g == 0)
    slots = min(2, velocities // group)
    return pl.pallas_call(
        stack_kernel,
        out_shape=jax.ShapeDtypeStruct((velocities, LANES * per, LANES), jnp.float32),
        in_specs=[smem, vmem, vmem],
        out_specs=pl.BlockSpec(memory_space=pl.ANY),
        scratch_shapes=[
            pltpu.VMEM((slots, group, LANES * per, LANES), jnp.float32),
            pltpu.SemaphoreType.DMA((slots, group)),
        ],
        compiler_params=pltpu.CompilerParams(vmem_limit_bytes=8 * 2**20),
        name="stack",
    )(shifts.transpose(1, 2, 0), kernel, held)


def local(images, variance, spread_kernel, shifts, epoch_owner, valid_rows):
    band, columns = images.shape[1:]
    blocks = columns // LANES
    groups = LANES // blocks
    per = band // groups

    def tiled(array):
        return array.reshape(groups, per, blocks, LANES).transpose(0, 2, 1, 3).reshape(-1, LANES)

    held = search(tiled(images), tiled(variance), spread_kernel, epoch_owner, valid_rows, blocks)
    out = stack(held, shifts, spread_kernel)
    out = out.reshape(-1, groups, blocks, per, LANES).transpose(0, 1, 3, 2, 4)
    return out.reshape(-1, band, columns)


def solution(mesh):
    in_specs = (
        P(("fields", "vel"), "rows", None),
        P(("fields", "vel"), "rows", None),
        P(),
        P(("fields", "vel"), None, None),
        P("fields"),
        P("fields", None),
    )
    out_specs = P(("fields", "vel"), "rows", None)
    return jax.shard_map(local, mesh=mesh, in_specs=in_specs, out_specs=out_specs, check_vma=False)
```
